32 devices in a mesh: tm: 2 (over core), rows: 16 (over z, y, x).
Axes of the slice: x: 2, y: 2, z: 4, core: 2. Of those that a mesh axis runs over, the one named last changes fastest.
Arguments:
- tiles: bfloat16 [2, 128, 128, 128], P('tm', 'rows'), may hold values from -0.125 to 0.125
- tile_cols: int32 [2, 128], P('tm', 'rows'), may hold values from 0 to 15, as said below
- tile_count: int32 [2, 16], P('tm', 'rows'), may hold values from 4 to 8, as said below
- start_right: bfloat16 [2, 2048, 256], P('tm', 'rows'), may hold values from -48 to 48
Outputs:
- left_embed: float32 [2048, 256], P('rows')
- right_embed: float32 [2, 2048, 256], P('tm', 'rows')
The draws below stay inside these ranges and needn't reach their ends.
Inputs may be any that keep to these rules, and one draw needn't show every extreme that they name: `tile_cols`: within one row block of one snapshot the 8 slots name distinct column blocks. `tile_count`: some row block of some snapshot has all 8 slots live in every draw.
All inputs are finite; a program needn't handle non-finite values.
Results may differ from the reference program's by a relative error of at most 0.0027.
Values may be sent and summed in bfloat16 or wider, within the bound.
A program may use at most 64 MiB of HBM per device.

```python
import math
import jax
import jax.numpy as jnp
from jax import lax

BLOCK = 128
COLS = 256
ITERS = 1
SNAPS = 2
BLOCKS = 16
TILES_DEV = 8
NODES = 2048


def draw_tile_count(key, part):
    first, second = jax.random.split(key)
    counts = jax.random.randint(first, (SNAPS * BLOCKS,), (TILES_DEV + 1) // 2, TILES_DEV + 1)
    where_full = jax.random.randint(second, (), 0, SNAPS * BLOCKS)
    counts = counts.at[where_full].set(TILES_DEV)
    return counts.reshape(SNAPS, BLOCKS).astype(jnp.int32)


def pick_columns(one_key):
    return jax.random.permutation(one_key, BLOCKS)[:TILES_DEV]


def draw_tile_cols(key, part):
    keys = jax.random.split(jax.random.fold_in(key, 7), SNAPS * BLOCKS)
    chosen = jax.vmap(pick_columns)(keys)
    return chosen.reshape(SNAPS, BLOCKS * TILES_DEV).astype(jnp.int32)


def draw_start_right(key, part):
    first, second = jax.random.split(jax.random.fold_in(key, 11), 2)
    shape = (SNAPS, NODES, COLS)
    base = jnp.clip(jax.random.normal(first, shape, jnp.float32), -4.0, 4.0)
    scale = jnp.exp(jax.random.uniform(second, (SNAPS, NODES, 1), jnp.float32) * jnp.log(10.0))
    return jnp.clip(base * scale, -48.0, 48.0).astype(jnp.bfloat16)


def steps_of(key, shape, shards, least, top_value):
    factor_of = 1.0
    for dim, shards_of in shards:
        draws = jax.random.uniform(jax.random.fold_in(jax.random.fold_in(key, 6), dim), (shards_of,), jnp.float32, least / len(shards), top_value / len(shards))
        factor_of = factor_of * jnp.repeat(jnp.exp(draws), shape[dim] // shards_of).reshape((-1,) + (1,) * (len(shape) - 1 - dim))
    return factor_of


def normal_values(rng, extent, scale, limit, cuts=(), held_as=jnp.bfloat16):
    values = scale * jax.random.normal(rng, extent, jnp.float32)
    if cuts:
        values = values * steps_of(rng, extent, cuts, -0.22, 0.18)
    return jnp.clip(values, -limit, limit).astype(held_as)


def setup_inputs(seed: int = 0) -> dict:
    key_list = jax.random.split(jax.random.key(seed), 5)
    return {
        "tiles": normal_values(key_list[0], (SNAPS, BLOCKS * TILES_DEV, BLOCK, BLOCK), (SNAPS * TILES_DEV * BLOCK) ** -0.5, 0.125, ((0, 2), (1, 16))),
        "tile_cols": draw_tile_cols(jax.random.fold_in(key_list[4], 71), 0),
        "tile_count": draw_tile_count(jax.random.fold_in(key_list[4], 71), 0),
        "start_right": draw_start_right(jax.random.fold_in(key_list[4], 71), 0),
    }


def orthonormal(values, gram, total):
    factor = jnp.linalg.cholesky(gram)
    solved = lax.linalg.triangular_solve(factor, values, left_side=False, lower=True, transpose_a=True)
    return solved * math.sqrt(total)

def reference(tiles, tile_cols, tile_count, start_right):
    slots = jnp.arange(TILES_DEV, dtype=jnp.int32)
    live = (slots[None, None, :] < tile_count[:, :, None]).reshape(SNAPS, BLOCKS * TILES_DEV)
    masked = jnp.where(live[:, :, None, None], tiles, jnp.zeros_like(tiles))
    placing = (tile_cols[:, :, None] == jnp.arange(BLOCKS, dtype=jnp.int32)[None, None, :]).astype(jnp.float32)
    current = start_right
    left_embed = jnp.zeros((NODES, COLS), jnp.float32)
    right_embed = jnp.zeros((SNAPS, NODES, COLS), jnp.float32)
    for step in range(ITERS):

        def left_term(items):
            tile_set, columns, right_now = items
            picked = right_now.reshape(BLOCKS, BLOCK, COLS)[columns.astype(jnp.int32)]
            prods = jnp.einsum('sij,sjk->sik', tile_set.astype(jnp.float32), picked.astype(jnp.float32))
            return prods.reshape(BLOCKS, TILES_DEV, BLOCK, COLS).sum(axis=1).reshape(NODES, COLS)
        terms = lax.map(left_term, (masked, tile_cols, current))
        summed = lax.optimization_barrier(jnp.sum(terms, axis=0))
        gram = jnp.dot(summed.T, summed, precision=lax.Precision.HIGHEST)
        left_embed = orthonormal(summed, gram, NODES)
        basis = left_embed.astype(jnp.bfloat16).astype(jnp.float32).reshape(BLOCKS, BLOCK, COLS)

        def right_term(items):
            tile_set, place = items
            grouped = tile_set.reshape(BLOCKS, TILES_DEV, BLOCK, BLOCK).astype(jnp.float32)
            pieces = jnp.einsum('rsij,rik->rsjk', grouped, basis)
            placed = jnp.einsum('sc,sjk->cjk', place, pieces.reshape(BLOCKS * TILES_DEV, BLOCK, COLS))
            return placed.reshape(NODES, COLS)
        image = lax.map(right_term, (masked, placing))
        stacked = image.reshape(SNAPS * NODES, COLS)
        rgram = jnp.dot(stacked.T, stacked, precision=lax.Precision.HIGHEST)
        right_embed = orthonormal(stacked, rgram, SNAPS * NODES).reshape(SNAPS, NODES, COLS)
        current = right_embed.astype(jnp.bfloat16)
    return (left_embed, right_embed)
```

```python
import functools
import math

import jax
import jax.numpy as jnp
from jax import lax
from jax.experimental import pallas as pl
from jax.experimental.pallas import tpu as pltpu
from jax.sharding import PartitionSpec as P

BLOCK = 128
COLS = 256
PLANE = 4
WIDE = 16
MESH = pl.DeviceIdType.MESH
HIGHEST = lax.Precision.HIGHEST


def dot_tn(a, b, precision=None):
    return lax.dot_general(
        a, b, (((0,), (0,)), ((), ())), precision=precision, preferred_element_type=jnp.float32
    )


def dot_nt(a, b):
    return lax.dot_general(
        a, b, (((1,), (1,)), ((), ())), precision=HIGHEST, preferred_element_type=jnp.float32
    )


def exchange(
    nrows, nsnaps, slots, owners,
    cols_hbm, count_hbm, tiles_hbm, x_hbm,
    left_ref, image_ref, rgram_ref,
    cols_ref, count_ref, sum_ref, gram_ref, tiles_ref, out_tiles, in_tiles, x_all, parts, s_all, gpart, gpair, ghalf, gchunks,
    local_sem, f_send, f_recv, h_send, h_recv, b_send, b_recv,
    x_send, x_recv, t_send, t_recv, p_send, p_recv, s_send, s_recv, c_send, c_recv,
    g_send, g_recv, r_send, r_recv,
):
    snap = lax.axis_index("tm")
    row = lax.axis_index("rows")
    total = nrows * nsnaps
    flat = snap * nrows + row
    half = COLS // nsnaps
    chunk = half // owners
    piece = BLOCK // nsnaps

    def copy(src, dst, send, recv, to):
        return pltpu.make_async_remote_copy(
            src_ref=src, dst_ref=dst, send_sem=send, recv_sem=recv,
            device_id=to, device_id_type=MESH,
        )

    def row_peer(k):
        return lax.rem(row + k, nrows)

    def snap_peer(k):
        return lax.rem(snap + k, nsnaps)

    def flat_peer(k):
        other = lax.rem(flat + k, total)
        return other, (other // nrows, lax.rem(other, nrows))

    tiles_in = pltpu.make_async_copy(tiles_hbm.at[0], tiles_ref, local_sem.at[0])
    x_in = pltpu.make_async_copy(x_hbm.at[0], x_all.at[row], local_sem.at[1])
    cols_in = pltpu.make_async_copy(cols_hbm, cols_ref, local_sem.at[2])
    count_in = pltpu.make_async_copy(count_hbm, count_ref, local_sem.at[3])
    barrier = pltpu.get_barrier_semaphore()

    @pl.loop(1, total)
    def _(k):
        pl.semaphore_signal(barrier, inc=1, device_id=flat_peer(k)[1], device_id_type=MESH)

    for c in (x_in, cols_in, count_in, tiles_in):
        c.start()
    for c in (cols_in, count_in, tiles_in):
        c.wait()

    @pl.loop(0, nrows)
    def _(c):
        slot = jnp.int32(0)
        present = jnp.int32(0)
        for s in range(slots):
            hit = jnp.logical_and(cols_ref[0, s] == c, s < count_ref[0, 0])
            slot = jnp.where(hit, s, slot)
            present = jnp.where(hit, 1, present)
        tile = tiles_ref[slot]
        out_tiles[c] = jnp.where(present > 0, tile, jnp.zeros_like(tile))

    in_tiles[row] = out_tiles[row]
    pl.semaphore_wait(barrier, total - 1)

    depth = nrows // PLANE
    level = row // PLANE
    place = lax.rem(row, PLANE)
    side = row + 1 - 2 * lax.rem(row, 2)
    flip = row + 2 - 4 * lax.rem(row // 2, 2)
    side_place, flip_place = lax.rem(side, PLANE), lax.rem(flip, PLANE)
    across_place = PLANE - 1 - place

    def relay(view, send, recv, on_arrival):
        def over(b, kind, at, slot_at, to, half=None):
            return copy(
                view(b, half), view(b, half), send.at[kind, slot_at], recv.at[kind, at], (snap, to)
            )

        def level_copy(k):
            to = lax.rem(level + k, depth)
            return over(row, 0, level, to, to * PLANE + place)

        def spread(v):
            b = v * PLANE + place
            return over(b, 1, v, v, side), over(b, 2, v, v, flip)

        def corner(v):
            return (
                over(v * PLANE + flip_place, 3, v, v, side, 0),
                over(v * PLANE + side_place, 4, v, v, flip, 1),
            )

        def arrived(kind, v, at_place, half=None):
            over(v * PLANE + at_place, kind, v, v, side, half).wait_recv()

        def forward(v):
            arrived(1, v, side_place)
            arrived(2, v, flip_place)
            for c in corner(v):
                c.start()
            on_arrival(v * PLANE + side_place)
            on_arrival(v * PLANE + flip_place)

        @pl.loop(1, depth)
        def _(k):
            level_copy(k).start()

        for c in spread(level):
            c.start()
        on_arrival(row)

        @pl.loop(1, depth)
        def _(k):
            v = lax.rem(level + depth - k, depth)
            arrived(0, v, place)
            for c in spread(v):
                c.start()
            on_arrival(v * PLANE + place)
            forward(lax.rem(v + 1, depth))

        forward(lax.rem(level + 1, depth))

        def corners(v):
            arrived(3, v, across_place, 0)
            arrived(4, v, across_place, 1)

        def finish():
            @pl.loop(1, depth)
            def _(k):
                level_copy(k).wait_send()

            @pl.loop(0, depth)
            def _(v):
                for c in spread(v) + corner(v):
                    c.wait_send()

        return corners, finish

    def x_view(b, half):
        if half is None:
            return x_all.at[b]
        return x_all.at[b, :, pl.ds(half * BLOCK, BLOCK)]

    def t_copy(src, k):
        return copy(
            out_tiles.at[row_peer(k)], in_tiles.at[src], t_send.at[k], t_recv.at[src],
            (snap, row_peer(k)),
        )

    x_in.wait()
    x_corners, x_finish = relay(x_view, x_send, x_recv, lambda b: None)

    @pl.loop(1, nrows)
    def _(k):
        t_copy(row, k).start()

    def level_at(k):
        return lax.rem(level + depth - k, depth)

    for k in range(depth):
        v = level_at(k)
        x_corners(v)
        first = v * PLANE
        tiles_of = jnp.concatenate([out_tiles[first + i] for i in range(PLANE)], axis=1)
        x_of = x_all[pl.ds(first, PLANE)].reshape(PLANE * BLOCK, COLS)
        value = jnp.dot(tiles_of, x_of, preferred_element_type=jnp.float32)
        if k:
            parts[snap] += value.reshape(nsnaps, piece, COLS)
        else:
            parts[snap] = value.reshape(nsnaps, piece, COLS)

    def p_copy(src, to, k):
        return copy(
            parts.at[src, to], parts.at[src, to], p_send.at[k], p_recv.at[src], (to, row)
        )

    for k in range(1, nsnaps):
        p_copy(snap, snap_peer(k), k).start()
    for k in range(1, nsnaps):
        p_copy(snap_peer(k), snap, k).wait_recv()
    summed = parts[0, snap]
    for k in range(1, nsnaps):
        summed = summed + parts[k, snap]
    sum_ref[snap] = summed
    s_all[row, snap] = summed.astype(jnp.bfloat16)

    def s_view(b, half):
        if half is None:
            return s_all.at[b, snap]
        return s_all.at[b, snap, :, pl.ds(half * BLOCK, BLOCK)]

    def share(b, k):
        return copy(
            s_all.at[b, snap], s_all.at[b, snap], c_send.at[k, b], c_recv.at[snap, b],
            (snap_peer(k), row),
        )

    def share_all(b):
        for k in range(1, nsnaps):
            share(b, k).start()

    s_corners, s_finish = relay(s_view, s_send, s_recv, share_all)

    def f_copy(src, to, k):
        return copy(sum_ref.at[src], sum_ref.at[src], f_send.at[k], f_recv.at[src], (to, row))

    for k in range(1, nsnaps):
        f_copy(snap, snap_peer(k), k).start()

    @pl.loop(1, nrows)
    def _(k):
        b = row_peer(nrows - k)
        t_copy(b, k).wait_recv()

    for k in range(depth):
        v = level_at(k)
        first = v * PLANE
        s_corners(v)
        share_all(first + across_place)
        for i in range(PLANE):
            b = first + i
            for j in range(1, nsnaps):
                src = snap_peer(j)
                copy(
                    s_all.at[b, src], s_all.at[b, src], c_send.at[j, b], c_recv.at[src, b],
                    (src, row),
                ).wait_recv()
        got = s_all[pl.ds(first, PLANE)].reshape(PLANE * BLOCK, COLS)
        tiles_of = in_tiles[pl.ds(first, PLANE)].reshape(PLANE * BLOCK, BLOCK)
        gram_of, image_of = dot_tn(got, got), dot_tn(tiles_of, got)
        if k:
            gram_ref[...] += gram_of
            image_ref[...] += image_of
        else:
            gram_ref[...] = gram_of
            image_ref[...] = image_of

    image = image_ref[...]
    gpart[...] = dot_tn(image, image, HIGHEST)

    def rows_of(who, count):
        return pl.ds(pl.multiple_of(who * count, count), count)

    def h_copy(src, to, k):
        return copy(
            gpart.at[rows_of(to, half)], gpair.at[src], h_send.at[k], h_recv.at[src], (to, row)
        )

    for k in range(1, nsnaps):
        h_copy(snap, snap_peer(k), k).start()
    for k in range(1, nsnaps):
        h_copy(snap_peer(k), snap, k).wait_recv()
    mine = gpart[rows_of(snap, half), :]
    for k in range(1, nsnaps):
        mine = mine + gpair[snap_peer(k)]
    ghalf[...] = mine

    def g_copy(src, k, who):
        return copy(
            ghalf.at[rows_of(who, chunk)], gchunks.at[src], g_send.at[k], g_recv.at[src],
            (snap, who),
        )

    def result(of_snap, of_row):
        at = pl.multiple_of(of_snap * half + of_row * chunk, chunk)
        return rgram_ref.at[pl.ds(at, chunk)]

    def r_copy(src, k, to):
        return copy(result(snap, src), result(snap, src), r_send.at[k], r_recv.at[src], (snap, to))

    def b_copy(of_snap, of_row, to, k):
        return copy(
            result(of_snap, of_row), result(of_snap, of_row), b_send.at[k, of_row],
            b_recv.at[of_snap, of_row], (to, row),
        )

    def if_owner(who, body):
        if owners == nrows:
            body()
        else:
            pl.when(who < owners)(body)

    @pl.loop(1, nrows)
    def _(k):
        who = row_peer(k)
        if_owner(who, lambda: g_copy(row, k, who).start())

    left = Whiten(gram_ref)
    left.first()
    for i in range(1, nsnaps):
        f_copy(snap_peer(i), snap, i).wait_recv()

    def reduce_own():
        def step(k, acc):
            src = row_peer(nrows - k)
            g_copy(src, k, row).wait_recv()
            return acc + gchunks[src]

        acc = lax.fori_loop(1, nrows, step, ghalf[rows_of(row, chunk), :])
        at = pl.multiple_of(snap * half + row * chunk, chunk)
        rgram_ref[pl.ds(at, chunk), :] = acc

        @pl.loop(1, nrows)
        def _(k):
            r_copy(row, k, row_peer(k)).start()

        for k in range(1, nsnaps):
            b_copy(snap, row, snap_peer(k), k).start()

    if_owner(row, reduce_own)

    left.second(sum_ref[...].reshape(BLOCK, COLS), left_ref, math.sqrt(nrows * BLOCK))

    @pl.loop(1, nrows)
    def _(k):
        src = row_peer(nrows - k)

        def pass_on():
            r_copy(src, k, row).wait_recv()
            for i in range(1, nsnaps):
                b_copy(snap, src, snap_peer(i), i).start()

        if_owner(src, pass_on)

    @pl.loop(0, owners)
    def _(src):
        for i in range(1, nsnaps):
            b_copy(snap_peer(i), src, snap, i).wait_recv()

    x_finish()
    s_finish()

    @pl.loop(0, nrows)
    def _(b):
        for i in range(1, nsnaps):
            share(b, i).wait_send()

    @pl.loop(0, owners)
    def _(src):
        for i in range(1, nsnaps):
            b_copy(snap, src, snap_peer(i), i).wait_send()

    for k in range(1, nsnaps):
        p_copy(snap, snap_peer(k), k).wait_send()
        f_copy(snap, snap_peer(k), k).wait_send()
        h_copy(snap, snap_peer(k), k).wait_send()

    @pl.loop(1, nrows)
    def _(k):
        t_copy(row, k).wait_send()
        who = row_peer(k)
        if_owner(who, lambda: g_copy(row, k, who).wait_send())
        if_owner(row, lambda: r_copy(row, k, who).wait_send())


def eliminate(matrix):
    lane = lax.broadcasted_iota(jnp.int32, (8, BLOCK), 1)
    sub = lax.broadcasted_iota(jnp.int32, (8, BLOCK), 0)
    groups = BLOCK // 8
    across = lambda v, j: jnp.broadcast_to(v[:, j : j + 1], (8, BLOCK))
    down = lambda v, i: jnp.broadcast_to(v[i : i + 1, :], (8, BLOCK))
    z = [matrix[8 * g : 8 * g + 8, :] for g in range(groups)]
    halves = range(WIDE // 8)
    for g0 in range(0, groups, WIDE // 8):
        j0 = 8 * g0
        inside = jnp.logical_and(lane >= j0, lane < j0 + WIDE)
        panel = [[across(z[g0 + s], j0 + q) for s in halves] for q in range(WIDE)]
        both = [
            jnp.where(inside, jnp.where(lane == sub + (j0 + 8 * s), 1.0, 0.0), z[g0 + s])
            for s in halves
        ]
        kept = list(both)
        inverse = [jnp.zeros((8, BLOCK), jnp.float32) for s in halves]
        for p in range(WIDE):
            ps, pi = p // 8, p % 8
            here = sub == pi
            recip = 1.0 / down(panel[p][ps], pi)
            inverse[ps] = jnp.where(here, recip, inverse[ps])
            column = list(panel[p])
            column[ps] = jnp.where(here, 0.0, column[ps])
            factor = [c * recip for c in column]
            for q in range(p + 1, WIDE):
                d = down(panel[q][ps], pi)
                for s in halves:
                    step = (column[s] * d) * recip if q == p + 1 else factor[s] * d
                    panel[q][s] = panel[q][s] - step
            pivot_row = down(both[ps], pi)
            kept[ps] = jnp.where(here, pivot_row, kept[ps])
            for s in halves:
                both[s] = both[s] - factor[s] * pivot_row
        rows = [down(both[q // 8] * inverse[q // 8], q % 8) for q in range(WIDE)]
        for s in halves:
            z[g0 + s] = kept[s] * jnp.sqrt(inverse[s])
        for g in range(g0 + WIDE // 8, groups):
            new = jnp.where(inside, 0.0, z[g])
            for q in range(WIDE):
                new = new - across(z[g], j0 + q) * rows[q]
            z[g] = new
    return jnp.concatenate(
        [jnp.where(lane <= sub + 8 * g, z[g], 0.0) for g in range(groups)], axis=0
    )


class Whiten:
    def __init__(self, gram):
        self.gram = gram

    def first(self):
        lo, hi = slice(0, BLOCK), slice(BLOCK, COLS)
        self.upper = eliminate(self.gram[lo, lo])
        self.below = dot_nt(self.gram[hi, lo], self.upper)
        self.rest = self.gram[hi, hi] - dot_nt(self.below, self.below)

    def second(self, values, out, scale):
        lo, hi = slice(0, BLOCK), slice(BLOCK, COLS)
        head = dot_nt(values[:, lo], self.upper)
        tail = values[:, hi] - dot_nt(head, self.below)
        lower = eliminate(self.rest)
        out[:, lo] = head * scale
        out[:, hi] = dot_nt(tail, lower) * scale


def whiten(scale, left_in, image_ref, rgram_ref, left_out, right_ref, sem):
    copy = pltpu.make_async_copy(left_in, left_out, sem)
    copy.start()
    right = Whiten(rgram_ref)
    right.first()
    right.second(image_ref[...], right_ref, scale)
    copy.wait()


def on_device(tiles, tile_cols, tile_count, start_right):
    nrows = lax.axis_size("rows")
    nsnaps = lax.axis_size("tm")
    nodes = BLOCK * nrows
    slots = tiles.shape[1]
    owners = min(nrows, COLS // nsnaps // 8)
    f32, bf16 = jnp.float32, jnp.bfloat16
    vmem = pl.BlockSpec(memory_space=pltpu.VMEM)
    hbm = pl.BlockSpec(memory_space=pltpu.HBM)
    dma = lambda *n: pltpu.SemaphoreType.DMA(n)
    block = jax.ShapeDtypeStruct((BLOCK, COLS), f32)
    square = jax.ShapeDtypeStruct((COLS, COLS), f32)
    left, image, rgram = pl.pallas_call(
        functools.partial(exchange, nrows, nsnaps, slots, owners),
        out_shape=(block, block, square),
        in_specs=[hbm] * 4,
        out_specs=(vmem,) * 3,
        scratch_shapes=[
            pltpu.SMEM(tile_cols.shape, jnp.int32),
            pltpu.SMEM(tile_count.shape, jnp.int32),
            pltpu.VMEM((nsnaps, BLOCK // nsnaps, COLS), f32),
            pltpu.VMEM((COLS, COLS), f32),
            pltpu.VMEM((slots, BLOCK, BLOCK), bf16),
            pltpu.VMEM((nrows, BLOCK, BLOCK), bf16),
            pltpu.VMEM((nrows, BLOCK, BLOCK), bf16),
            pltpu.VMEM((nrows, BLOCK, COLS), bf16),
            pltpu.VMEM((nsnaps, nsnaps, BLOCK // nsnaps, COLS), f32),
            pltpu.VMEM((nrows, nsnaps, BLOCK // nsnaps, COLS), bf16),
            pltpu.VMEM((COLS, COLS), f32),
            pltpu.VMEM((nsnaps, COLS // nsnaps, COLS), f32),
            pltpu.VMEM((COLS // nsnaps, COLS), f32),
            pltpu.VMEM((nrows, COLS // nsnaps // owners, COLS), f32),
            dma(4), dma(nsnaps), dma(nsnaps), dma(nsnaps), dma(nsnaps),
            dma(nsnaps, nrows), dma(nsnaps, nrows),
            dma(5, nrows // PLANE), dma(5, nrows // PLANE), dma(nrows), dma(nrows),
            dma(nsnaps), dma(nsnaps), dma(5, nrows // PLANE), dma(5, nrows // PLANE),
            dma(nsnaps, nrows), dma(nsnaps, nrows),
            dma(nrows), dma(nrows), dma(nrows), dma(nrows),
        ],
        compiler_params=pltpu.CompilerParams(
            collective_id=0, has_side_effects=True, vmem_limit_bytes=48 * 1024 * 1024
        ),
        name="exchange",
    )(tile_cols, tile_count, tiles, start_right)
    left, right = pl.pallas_call(
        functools.partial(whiten, math.sqrt(nodes * nsnaps)),
        out_shape=(block, block),
        in_specs=[vmem] * 3,
        out_specs=(hbm, vmem),
        scratch_shapes=[pltpu.SemaphoreType.DMA],
        compiler_params=pltpu.CompilerParams(vmem_limit_bytes=32 * 1024 * 1024),
        name="whiten",
    )(left, image, rgram)
    return (left, right[None])


def solution(mesh):
    placed = (P("tm", "rows", None, None), P("tm", "rows"), P("tm", "rows"), P("tm", "rows", None))
    return jax.shard_map(
        on_device,
        mesh=mesh,
        in_specs=placed,
        out_specs=(P("rows", None), P("tm", "rows", None)),
        check_vma=False,
    )
```

```python
import functools
import math

import jax
import jax.numpy as jnp
from jax import lax
from jax.experimental import pallas as pl
from jax.experimental.pallas import tpu as pltpu
from jax.sharding import PartitionSpec as P

BLOCK = 128
COLS = 256
PLANE = 4
WIDE = 16
MESH = pl.DeviceIdType.MESH
HIGHEST = lax.Precision.HIGHEST


def dot_nn(a, b):
    return jnp.dot(a, b, preferred_element_type=jnp.float32)


def dot_tn(a, b, precision=None):
    return lax.dot_general(
        a, b, (((0,), (0,)), ((), ())), precision=precision, preferred_element_type=jnp.float32
    )


def dot_nt(a, b):
    return lax.dot_general(
        a, b, (((1,), (1,)), ((), ())), precision=HIGHEST, preferred_element_type=jnp.float32
    )


def remote(src, dst, send, recv, to):
    return pltpu.make_async_remote_copy(
        src_ref=src, dst_ref=dst, send_sem=send, recv_sem=recv, device_id=to, device_id_type=MESH
    )


class Elimination:
    def __init__(self, matrix):
        self.z = [matrix[8 * g : 8 * g + 8, :] for g in range(BLOCK // 8)]
        self.at = 0

    def run(self, steps=BLOCK // WIDE):
        lane = lax.broadcasted_iota(jnp.int32, (8, BLOCK), 1)
        sub = lax.broadcasted_iota(jnp.int32, (8, BLOCK), 0)
        across = lambda v, j: jnp.broadcast_to(v[:, j : j + 1], (8, BLOCK))
        down = lambda v, i: jnp.broadcast_to(v[i : i + 1, :], (8, BLOCK))
        z, halves = self.z, range(WIDE // 8)
        for _ in range(steps):
            g0 = self.at
            self.at += WIDE // 8
            j0 = 8 * g0
            inside = jnp.logical_and(lane >= j0, lane < j0 + WIDE)
            panel = [[across(z[g0 + s], j0 + q) for s in halves] for q in range(WIDE)]
            both = [
                jnp.where(inside, jnp.where(lane == sub + (j0 + 8 * s), 1.0, 0.0), z[g0 + s])
                for s in halves
            ]
            kept = list(both)
            inverse = [jnp.zeros((8, BLOCK), jnp.float32) for s in halves]
            for p in range(WIDE):
                ps, pi = p // 8, p % 8
                here = sub == pi
                recip = 1.0 / down(panel[p][ps], pi)
                inverse[ps] = jnp.where(here, recip, inverse[ps])
                column = list(panel[p])
                column[ps] = jnp.where(here, 0.0, column[ps])
                factor = [c * recip for c in column]
                for q in range(p + 1, WIDE):
                    d = down(panel[q][ps], pi)
                    for s in halves:
                        step = (column[s] * d) * recip if q == p + 1 else factor[s] * d
                        panel[q][s] = panel[q][s] - step
                pivot_row = down(both[ps], pi)
                kept[ps] = jnp.where(here, pivot_row, kept[ps])
                for s in halves:
                    both[s] = both[s] - factor[s] * pivot_row
            rows = [down(both[q // 8] * inverse[q // 8], q % 8) for q in range(WIDE)]
            for s in halves:
                z[g0 + s] = kept[s] * jnp.sqrt(inverse[s])
            for g in range(g0 + WIDE // 8, BLOCK // 8):
                new = jnp.where(inside, 0.0, z[g])
                for q in range(WIDE):
                    new = new - across(z[g], j0 + q) * rows[q]
                z[g] = new
        return self

    def result(self):
        lane = lax.broadcasted_iota(jnp.int32, (8, BLOCK), 1)
        sub = lax.broadcasted_iota(jnp.int32, (8, BLOCK), 0)
        return jnp.concatenate(
            [jnp.where(lane <= sub + 8 * g, z, 0.0) for g, z in enumerate(self.z)], axis=0
        )


class Total:
    def __init__(self, refs, sems, place):
        self.part, self.pair, self.mine, self.chunks, self.result = refs
        self.hs, self.hr, self.gs, self.gr, self.rs, self.rr, self.bs, self.br = sems
        self.snap, self.row, self.nsnaps, self.nrows = place
        self.half = self.part.shape[0] // self.nsnaps
        self.chunk = self.chunks.shape[1]
        self.owners = self.half // self.chunk
        self.first = (self.nrows - self.owners) // 2

    def snap_peer(self, k):
        return lax.rem(self.snap + k, self.nsnaps)

    def h_copy(self, src, to, k):
        at = pl.ds(pl.multiple_of(to * self.half, self.half), self.half)
        return remote(
            self.part.at[at], self.pair.at[src], self.hs.at[k], self.hr.at[src], (to, self.row)
        )

    def g_copy(self, src, owner):
        at = pl.ds(pl.multiple_of(owner * self.chunk, self.chunk), self.chunk)
        return remote(
            self.mine.at[at], self.chunks.at[src], self.gs.at[owner], self.gr.at[src],
            (self.snap, self.first + owner),
        )

    def r_copy(self, owner, to):
        at = pl.multiple_of(self.snap * self.half + owner * self.chunk, self.chunk)
        view = self.result.at[pl.ds(at, self.chunk)]
        return remote(view, view, self.rs.at[to], self.rr.at[owner], (self.snap, to))

    def b_copy(self, src, to, k):
        view = self.result.at[pl.ds(pl.multiple_of(src * self.half, self.half), self.half)]
        return remote(view, view, self.bs.at[k], self.br.at[src], (to, self.row))

    def if_owner(self, body):
        if self.owners == self.nrows:
            body()
        else:
            mine = jnp.logical_and(self.row >= self.first, self.row < self.first + self.owners)
            pl.when(mine)(body)

    def each_owner(self, body):
        @pl.loop(0, self.owners)
        def _(o):
            owner = lax.rem(o + self.row, self.owners)
            pl.when(self.first + owner != self.row)(lambda: body(owner))

    def pairs(self):
        for k in range(1, self.nsnaps):
            self.h_copy(self.snap, self.snap_peer(k), k).start()

    def scatter(self):
        for k in range(1, self.nsnaps):
            self.h_copy(self.snap_peer(k), self.snap, k).wait_recv()
        at = pl.ds(pl.multiple_of(self.snap * self.half, self.half), self.half)
        mine = self.part[at, :]
        for k in range(1, self.nsnaps):
            mine = mine + self.pair[self.snap_peer(k)]
        self.mine[...] = mine
        self.each_owner(lambda owner: self.g_copy(self.row, owner).start())

    def reduce(self):
        def body():
            owner = self.row - self.first
            at = pl.ds(pl.multiple_of(owner * self.chunk, self.chunk), self.chunk)

            def step(k, acc):
                src = lax.rem(self.row + self.nrows - k, self.nrows)
                self.g_copy(src, owner).wait_recv()
                return acc + self.chunks[src]

            acc = lax.fori_loop(1, self.nrows, step, self.mine[at, :])
            at = pl.multiple_of(self.snap * self.half + owner * self.chunk, self.chunk)
            self.result[pl.ds(at, self.chunk), :] = acc

            @pl.loop(1, self.nrows)
            def _(k):
                self.r_copy(owner, lax.rem(self.row + k, self.nrows)).start()

        self.if_owner(body)

    def share(self):
        self.each_owner(lambda owner: self.r_copy(owner, self.row).wait_recv())
        for k in range(1, self.nsnaps):
            self.b_copy(self.snap, self.snap_peer(k), k).start()

    def arrive(self):
        for k in range(1, self.nsnaps):
            self.b_copy(self.snap_peer(k), self.snap, k).wait_recv()

    def finish(self):
        for k in range(1, self.nsnaps):
            self.h_copy(self.snap, self.snap_peer(k), k).wait_send()
            self.b_copy(self.snap, self.snap_peer(k), k).wait_send()
        self.each_owner(lambda owner: self.g_copy(self.row, owner).wait_send())

        def body():
            @pl.loop(1, self.nrows)
            def _(k):
                self.r_copy(self.row - self.first, lax.rem(self.row + k, self.nrows)).wait_send()

        self.if_owner(body)


class Relay:
    def __init__(self, view, send, recv, place):
        self.view, self.send, self.recv = view, send, recv
        self.snap, self.row, self.nrows = place
        self.depth = self.nrows // PLANE
        self.level, self.place = self.row // PLANE, lax.rem(self.row, PLANE)
        side = self.place + 1 - 2 * lax.rem(self.place, 2)
        self.places = (side, PLANE - 1 - side, PLANE - 1 - self.place)

    def over(self, b, kind, at, slot, to):
        view = self.view(b)
        return remote(view, view, self.send.at[kind, slot], self.recv.at[kind, at], (self.snap, to))

    def level_copy(self, k):
        to = lax.rem(self.level + k, self.depth)
        return self.over(self.row, 0, self.level, to, to * PLANE + self.place)

    def spread(self, v):
        b = v * PLANE + self.place
        return [
            self.over(b, 1 + i, v, v, self.level * PLANE + p) for i, p in enumerate(self.places)
        ]

    def level_at(self, k):
        return lax.rem(self.level + self.depth - k, self.depth)

    def begin(self):
        @pl.loop(1, self.depth)
        def _(k):
            self.level_copy(k).start()

        for c in self.spread(self.level):
            c.start()

    def forward(self):
        @pl.loop(1, self.depth)
        def _(k):
            v = self.level_at(k)
            self.over(v * PLANE + self.place, 0, v, v, self.row).wait_recv()
            for c in self.spread(v):
                c.start()

    def arrive(self, v):
        for i, p in enumerate(self.places):
            self.over(v * PLANE + p, 1 + i, v, v, self.row).wait_recv()

    def finish(self):
        @pl.loop(1, self.depth)
        def _(k):
            self.level_copy(k).wait_send()

        @pl.loop(0, self.depth)
        def _(v):
            for c in self.spread(v):
                c.wait_send()


def embed(
    nrows, nsnaps, slots,
    cols_hbm, count_hbm, tiles_hbm, x_hbm,
    left_ref, right_ref,
    cols_ref, count_ref, tiles_ref, out_tiles, in_tiles, x_all, parts, sums, s_all, image_ref,
    part0, pair0, mine0, chunks0, total0, part1, pair1, mine1, chunks1, total1,
    local_sem, t_send, t_recv, p_send, p_recv, f_send, f_recv, c_send, c_recv,
    x_send0, x_recv0, x_send1, x_recv1, s_send0, s_recv0, s_send1, s_recv1, *total_sems,
):
    snap = lax.axis_index("tm")
    row = lax.axis_index("rows")
    everyone = nrows * nsnaps
    flat = snap * nrows + row
    piece = BLOCK // nsnaps
    depth = nrows // PLANE
    level = row // PLANE
    halves = range(COLS // BLOCK)

    def snap_peer(k):
        return lax.rem(snap + k, nsnaps)

    def row_peer(k):
        return lax.rem(row + k, nrows)

    barrier = pltpu.get_barrier_semaphore()

    @pl.loop(1, everyone)
    def _(k):
        other = lax.rem(flat + k, everyone)
        pl.semaphore_signal(
            barrier, inc=1, device_id=(other // nrows, lax.rem(other, nrows)), device_id_type=MESH
        )

    x_in = [
        pltpu.make_async_copy(
            x_hbm.at[0, :, pl.ds(h * BLOCK, BLOCK)], x_all.at[h, row], local_sem.at[h]
        )
        for h in halves
    ]
    loads = [
        pltpu.make_async_copy(cols_hbm, cols_ref, local_sem.at[2]),
        pltpu.make_async_copy(count_hbm, count_ref, local_sem.at[3]),
        pltpu.make_async_copy(tiles_hbm.at[0], tiles_ref.at[pl.ds(0, slots)], local_sem.at[4]),
    ]
    for c in x_in + loads:
        c.start()
    tiles_ref[slots] = jnp.zeros((BLOCK, BLOCK), tiles_ref.dtype)
    for c in x_in:
        c.wait()

    spot = (snap, row, nrows)
    x_sems = ((x_send0, x_recv0), (x_send1, x_recv1))
    s_sems = ((s_send0, s_recv0), (s_send1, s_recv1))
    x_relay = [Relay(lambda b, h=h: x_all.at[h, b], *x_sems[h], spot) for h in halves]
    s_relay = [Relay(lambda b, h=h: s_all.at[h, snap, b], *s_sems[h], spot) for h in halves]

    pl.semaphore_wait(barrier, everyone - 1)
    for r in x_relay:
        r.begin()

    for c in loads:
        c.wait()
    live = [jnp.where(s < count_ref[0, 0], cols_ref[0, s], -1) for s in range(slots)]

    @pl.loop(0, nrows)
    def _(c):
        slot = jnp.int32(slots)
        for s in range(slots):
            slot = jnp.where(live[s] == c, s, slot)
        out_tiles[c] = tiles_ref[slot]

    in_tiles[row] = out_tiles[row]

    def t_copy(src, k):
        to = row_peer(k)
        return remote(
            out_tiles.at[to], in_tiles.at[src], t_send.at[k], t_recv.at[src], (snap, to)
        )

    x_relay[0].forward()

    @pl.loop(1, nrows)
    def _(k):
        t_copy(row, k).start()

    x_relay[1].forward()

    def p_copy(h, src, to, k):
        view = parts.at[h, src, to]
        return remote(view, view, p_send.at[h, k], p_recv.at[h, src], (to, row))

    def f_copy(h, src, to, k):
        view = sums.at[h, src]
        return remote(view, view, f_send.at[h, k], f_recv.at[h, src], (to, row))

    for h in halves:
        value = None
        for k in range(depth):
            v = lax.rem(level + depth - k, depth)
            x_relay[h].arrive(v)
            first = v * PLANE
            tiles_of = jnp.concatenate([out_tiles[first + i] for i in range(PLANE)], axis=1)
            term = dot_nn(tiles_of, x_all[h, pl.ds(first, PLANE)].reshape(PLANE * BLOCK, BLOCK))
            value = term if value is None else value + term
        parts[h, snap] = value.reshape(nsnaps, piece, BLOCK)
        for k in range(1, nsnaps):
            p_copy(h, snap, snap_peer(k), k).start()
        for k in range(1, nsnaps):
            p_copy(h, snap_peer(k), snap, k).wait_recv()
        summed = parts[h, 0, snap]
        for k in range(1, nsnaps):
            summed = summed + parts[h, k, snap]
        sums[h, snap] = summed
        s_all[h, snap, row] = summed.astype(jnp.bfloat16)
        s_relay[h].begin()

    for h in halves:
        s_relay[h].forward()

    def c_copy(h, src, v, to, k):
        view = s_all.at[h, src, pl.ds(v * PLANE, PLANE)]
        return remote(view, view, c_send.at[h, k, v], c_recv.at[h, src, v], (to, row))

    def share(h):
        @pl.loop(0, depth)
        def _(k):
            v = lax.rem(level + depth - k, depth)
            s_relay[h].arrive(v)
            for i in range(1, nsnaps):
                c_copy(h, snap, v, snap_peer(i), i).start()

    def shared(h):
        @pl.loop(0, depth)
        def _(v):
            for i in range(1, nsnaps):
                c_copy(h, snap_peer(i), v, snap, i).wait_recv()

    def s_of(h, t):
        return s_all[h, t].reshape(nrows * piece, BLOCK)

    def tiles_at(t):
        return in_tiles[:, t * piece : (t + 1) * piece, :].reshape(nrows * piece, BLOCK)

    def image_of(h):
        return functools.reduce(
            jnp.add, [dot_tn(tiles_at(t), s_of(h, t)) for t in range(nsnaps)]
        )

    def gram_of(g, h):
        return functools.reduce(jnp.add, [dot_tn(s_of(g, t), s_of(h, t)) for t in range(nsnaps)])

    where = (snap, row, nsnaps, nrows)
    first_total = Total((part0, pair0, mine0, chunks0, total0), total_sems[:8], where)
    other_total = Total((part1, pair1, mine1, chunks1, total1), total_sems[8:], where)
    lo, hi = slice(0, BLOCK), slice(BLOCK, COLS)

    share(0)

    @pl.loop(1, nrows)
    def _(k):
        t_copy(row_peer(nrows - k), k).wait_recv()

    shared(0)
    image = image_of(0)
    image_ref[0] = image
    part0[...] = dot_tn(image, image, HIGHEST)
    first_total.pairs()

    share(1)
    first_total.scatter()
    shared(1)
    image = image_of(1)
    image_ref[1] = image
    part1[lo, :] = dot_tn(image, image_ref[0], HIGHEST)
    part1[hi, :] = dot_tn(image, image, HIGHEST)
    other_total.pairs()

    for h in halves:
        for k in range(1, nsnaps):
            f_copy(h, snap, snap_peer(k), k).start()
    gram00, gram10, gram11 = gram_of(0, 0), gram_of(1, 0), gram_of(1, 1)
    other_total.scatter()
    first_total.reduce()

    upper = Elimination(gram00).run().result()
    other_total.reduce()
    for h in halves:
        for k in range(1, nsnaps):
            f_copy(h, snap_peer(k), snap, k).wait_recv()
    left_lo, left_hi = (sums[h].reshape(BLOCK, BLOCK) for h in halves)
    below = dot_nt(gram10, upper)
    left_head = dot_nt(left_lo, upper)
    left_tail = left_hi - dot_nt(left_head, below)
    left_lower = Elimination(gram11 - dot_nt(below, below)).run(4)
    left_scale = math.sqrt(nrows * BLOCK)
    left_ref[:, lo] = left_head * left_scale

    first_total.share()
    first_total.arrive()
    upper = Elimination(total0[...]).run().result()
    other_total.share()
    head = dot_nt(image_ref[0], upper)
    scale = math.sqrt(nsnaps * nrows * BLOCK)
    right_ref[:, lo] = head * scale
    other_total.arrive()
    below = dot_nt(total1[lo, :], upper)
    lower = Elimination(total1[hi, :] - dot_nt(below, below)).run().result()
    tail = image_ref[1] - dot_nt(head, below)
    right_ref[:, hi] = dot_nt(tail, lower) * scale
    left_ref[:, hi] = dot_nt(left_tail, left_lower.run(4).result()) * left_scale

    for r in x_relay + s_relay:
        r.finish()
    first_total.finish()
    other_total.finish()
    for h in halves:
        for k in range(1, nsnaps):
            p_copy(h, snap, snap_peer(k), k).wait_send()
            f_copy(h, snap, snap_peer(k), k).wait_send()

            @pl.loop(0, depth)
            def _(v):
                c_copy(h, snap, v, snap_peer(k), k).wait_send()

    @pl.loop(1, nrows)
    def _(k):
        t_copy(row, k).wait_send()


def hand_over(left_in, right_in, left_out, right_out):
    left_out[...] = left_in[...]
    right_out[...] = right_in[...]


def on_device(tiles, tile_cols, tile_count, start_right):
    nrows = lax.axis_size("rows")
    nsnaps = lax.axis_size("tm")
    slots = tiles.shape[1]
    depth = nrows // PLANE
    piece = BLOCK // nsnaps
    f32, bf16 = jnp.float32, jnp.bfloat16
    vmem = pl.BlockSpec(memory_space=pltpu.VMEM)
    hbm = pl.BlockSpec(memory_space=pltpu.HBM)
    dma = lambda *n: pltpu.SemaphoreType.DMA(n)
    block = jax.ShapeDtypeStruct((BLOCK, COLS), f32)
    params = dict(vmem_limit_bytes=60 * 1024 * 1024)
    totals, total_sems = [], []
    for size in (BLOCK, 2 * BLOCK):
        half = size // nsnaps
        owners = min(nrows, half // 8)
        totals += [
            pltpu.VMEM((size, BLOCK), f32),
            pltpu.VMEM((nsnaps, half, BLOCK), f32),
            pltpu.VMEM((half, BLOCK), f32),
            pltpu.VMEM((nrows, half // owners, BLOCK), f32),
            pltpu.VMEM((size, BLOCK), f32),
        ]
        total_sems += [dma(nsnaps), dma(nsnaps)] + [dma(nrows)] * 4 + [dma(nsnaps), dma(nsnaps)]
    left, right = pl.pallas_call(
        functools.partial(embed, nrows, nsnaps, slots),
        out_shape=(block, block),
        in_specs=[hbm] * 4,
        out_specs=(vmem, vmem),
        scratch_shapes=[
            pltpu.SMEM(tile_cols.shape, jnp.int32),
            pltpu.SMEM(tile_count.shape, jnp.int32),
            pltpu.VMEM((slots + 1, BLOCK, BLOCK), bf16),
            pltpu.VMEM((nrows, BLOCK, BLOCK), bf16),
            pltpu.VMEM((nrows, BLOCK, BLOCK), bf16),
            pltpu.VMEM((2, nrows, BLOCK, BLOCK), bf16),
            pltpu.VMEM((2, nsnaps, nsnaps, piece, BLOCK), f32),
            pltpu.VMEM((2, nsnaps, piece, BLOCK), f32),
            pltpu.VMEM((2, nsnaps, nrows, piece, BLOCK), bf16),
            pltpu.VMEM((2, BLOCK, BLOCK), f32),
            *totals,
            dma(5), dma(nrows), dma(nrows),
            *[dma(2, nsnaps)] * 4,
            *[dma(2, nsnaps, depth)] * 2,
            *[dma(4, depth)] * 8,
            *total_sems,
        ],
        compiler_params=pltpu.CompilerParams(collective_id=0, has_side_effects=True, **params),
        name="embed",
    )(tile_cols, tile_count, tiles, start_right)
    left, right = pl.pallas_call(
        hand_over,
        out_shape=(block, block),
        in_specs=[vmem, vmem],
        out_specs=(vmem, vmem),
        compiler_params=pltpu.CompilerParams(**params),
        name="hand_over",
    )(left, right)
    return (left, right[None])


def solution(mesh):
    placed = (P("tm", "rows", None, None), P("tm", "rows"), P("tm", "rows"), P("tm", "rows", None))
    return jax.shard_map(
        on_device,
        mesh=mesh,
        in_specs=placed,
        out_specs=(P("rows", None), P("tm", "rows", None)),
        check_vma=False,
    )
```

```python
import functools
import math

import jax
import jax.numpy as jnp
from jax import lax
from jax.experimental import pallas as pl
from jax.experimental.pallas import tpu as pltpu
from jax.sharding import PartitionSpec as P

BLOCK = 128
COLS = 256
PLANE = 4
WIDE = 16
MESH = pl.DeviceIdType.MESH
HIGHEST = lax.Precision.HIGHEST


def dot_nn(a, b):
    return jnp.dot(a, b, preferred_element_type=jnp.float32)


def dot_tn(a, b, precision=None):
    return lax.dot_general(
        a, b, (((0,), (0,)), ((), ())), precision=precision, preferred_element_type=jnp.float32
    )


def dot_nt(a, b):
    return lax.dot_general(
        a, b, (((1,), (1,)), ((), ())), precision=HIGHEST, preferred_element_type=jnp.float32
    )


def remote(src, dst, send, recv, to):
    return pltpu.make_async_remote_copy(
        src_ref=src, dst_ref=dst, send_sem=send, recv_sem=recv, device_id=to, device_id_type=MESH
    )


class Elimination:
    def __init__(self, matrix):
        self.z = [matrix[8 * g : 8 * g + 8, :] for g in range(BLOCK // 8)]
        self.at = 0

    def run(self, steps=BLOCK // WIDE):
        lane = lax.broadcasted_iota(jnp.int32, (8, BLOCK), 1)
        sub = lax.broadcasted_iota(jnp.int32, (8, BLOCK), 0)
        across = lambda v, j: jnp.broadcast_to(v[:, j : j + 1], (8, BLOCK))
        down = lambda v, i: jnp.broadcast_to(v[i : i + 1, :], (8, BLOCK))
        z, halves = self.z, range(WIDE // 8)
        for _ in range(steps):
            g0 = self.at
            self.at += WIDE // 8
            j0 = 8 * g0
            inside = jnp.logical_and(lane >= j0, lane < j0 + WIDE)
            panel = [[across(z[g0 + s], j0 + q) for s in halves] for q in range(WIDE)]
            both = [
                jnp.where(inside, jnp.where(lane == sub + (j0 + 8 * s), 1.0, 0.0), z[g0 + s])
                for s in halves
            ]
            kept = list(both)
            inverse = [jnp.zeros((8, BLOCK), jnp.float32) for s in halves]
            for p in range(WIDE):
                ps, pi = p // 8, p % 8
                here = sub == pi
                recip = 1.0 / down(panel[p][ps], pi)
                inverse[ps] = jnp.where(here, recip, inverse[ps])
                column = list(panel[p])
                column[ps] = jnp.where(here, 0.0, column[ps])
                factor = [c * recip for c in column]
                for q in range(p + 1, WIDE):
                    d = down(panel[q][ps], pi)
                    for s in halves:
                        step = (column[s] * d) * recip if q == p + 1 else factor[s] * d
                        panel[q][s] = panel[q][s] - step
                pivot_row = down(both[ps], pi)
                kept[ps] = jnp.where(here, pivot_row, kept[ps])
                for s in halves:
                    both[s] = both[s] - factor[s] * pivot_row
            rows = [down(both[q // 8] * inverse[q // 8], q % 8) for q in range(WIDE)]
            for s in halves:
                z[g0 + s] = kept[s] * jnp.sqrt(inverse[s])
            for g in range(g0 + WIDE // 8, BLOCK // 8):
                new = jnp.where(inside, 0.0, z[g])
                for q in range(WIDE):
                    new = new - across(z[g], j0 + q) * rows[q]
                z[g] = new
        return self

    def result(self):
        lane = lax.broadcasted_iota(jnp.int32, (8, BLOCK), 1)
        sub = lax.broadcasted_iota(jnp.int32, (8, BLOCK), 0)
        return jnp.concatenate(
            [jnp.where(lane <= sub + 8 * g, z, 0.0) for g, z in enumerate(self.z)], axis=0
        )


class Total:
    def __init__(self, refs, sems, place):
        self.part, self.pair, self.mine, self.chunks, self.result = refs
        self.hs, self.hr, self.gs, self.gr, self.rs, self.rr, self.bs, self.br = sems
        self.snap, self.row, self.nsnaps, self.nrows = place
        self.half = self.part.shape[0] // self.nsnaps
        self.chunk = self.chunks.shape[1]
        self.owners = self.half // self.chunk
        self.first = (self.nrows - self.owners) // 2

    def snap_peer(self, k):
        return lax.rem(self.snap + k, self.nsnaps)

    def h_copy(self, src, to, k):
        at = pl.ds(pl.multiple_of(to * self.half, self.half), self.half)
        return remote(
            self.part.at[at], self.pair.at[src], self.hs.at[k], self.hr.at[src], (to, self.row)
        )

    def g_copy(self, src, owner):
        at = pl.ds(pl.multiple_of(owner * self.chunk, self.chunk), self.chunk)
        return remote(
            self.mine.at[at], self.chunks.at[src], self.gs.at[owner], self.gr.at[src],
            (self.snap, self.first + owner),
        )

    def r_copy(self, owner, to):
        at = pl.multiple_of(self.snap * self.half + owner * self.chunk, self.chunk)
        view = self.result.at[pl.ds(at, self.chunk)]
        return remote(view, view, self.rs.at[to], self.rr.at[owner], (self.snap, to))

    def b_copy(self, src, to, k):
        view = self.result.at[pl.ds(pl.multiple_of(src * self.half, self.half), self.half)]
        return remote(view, view, self.bs.at[k], self.br.at[src], (to, self.row))

    def if_owner(self, body):
        if self.owners == self.nrows:
            body()
        else:
            mine = jnp.logical_and(self.row >= self.first, self.row < self.first + self.owners)
            pl.when(mine)(body)

    def each_owner(self, body):
        @pl.loop(0, self.owners, unroll=self.nrows <= 16)
        def _(o):
            owner = lax.rem(o + self.row, self.owners)
            pl.when(self.first + owner != self.row)(lambda: body(owner))

    def pairs(self):
        for k in range(1, self.nsnaps):
            self.h_copy(self.snap, self.snap_peer(k), k).start()

    def scatter(self):
        for k in range(1, self.nsnaps):
            self.h_copy(self.snap_peer(k), self.snap, k).wait_recv()
        at = pl.ds(pl.multiple_of(self.snap * self.half, self.half), self.half)
        mine = self.part[at, :]
        for k in range(1, self.nsnaps):
            mine = mine + self.pair[self.snap_peer(k)]
        self.mine[...] = mine
        self.each_owner(lambda owner: self.g_copy(self.row, owner).start())

    def reduce(self):
        def body():
            owner = self.row - self.first
            at = pl.ds(pl.multiple_of(owner * self.chunk, self.chunk), self.chunk)

            def step(k, acc):
                src = lax.rem(self.row + self.nrows - k, self.nrows)
                self.g_copy(src, owner).wait_recv()
                return acc + self.chunks[src]

            acc = lax.fori_loop(1, self.nrows, step, self.mine[at, :], unroll=self.nrows <= 16)
            at = pl.multiple_of(self.snap * self.half + owner * self.chunk, self.chunk)
            self.result[pl.ds(at, self.chunk), :] = acc

            @pl.loop(1, self.nrows, unroll=self.nrows <= 16)
            def _(k):
                self.r_copy(owner, lax.rem(self.row + k, self.nrows)).start()

        self.if_owner(body)

    def share(self):
        self.each_owner(lambda owner: self.r_copy(owner, self.row).wait_recv())
        for k in range(1, self.nsnaps):
            self.b_copy(self.snap, self.snap_peer(k), k).start()

    def arrive(self):
        for k in range(1, self.nsnaps):
            self.b_copy(self.snap_peer(k), self.snap, k).wait_recv()

    def finish(self):
        for k in range(1, self.nsnaps):
            self.h_copy(self.snap, self.snap_peer(k), k).wait_send()
            self.b_copy(self.snap, self.snap_peer(k), k).wait_send()
        self.each_owner(lambda owner: self.g_copy(self.row, owner).wait_send())

        def body():
            @pl.loop(1, self.nrows, unroll=self.nrows <= 16)
            def _(k):
                self.r_copy(self.row - self.first, lax.rem(self.row + k, self.nrows)).wait_send()

        self.if_owner(body)


class Relay:
    def __init__(self, view, send, recv, place):
        self.view, self.send, self.recv = view, send, recv
        self.snap, self.row, self.nrows = place
        self.depth = self.nrows // PLANE
        self.level, self.place = self.row // PLANE, lax.rem(self.row, PLANE)
        side = self.place + 1 - 2 * lax.rem(self.place, 2)
        self.places = (side, PLANE - 1 - side, PLANE - 1 - self.place)

    def over(self, b, kind, at, slot, to):
        view = self.view(b)
        return remote(view, view, self.send.at[kind, slot], self.recv.at[kind, at], (self.snap, to))

    def level_copy(self, k):
        to = lax.rem(self.level + k, self.depth)
        return self.over(self.row, 0, self.level, to, to * PLANE + self.place)

    def spread(self, v):
        b = v * PLANE + self.place
        return [
            self.over(b, 1 + i, v, v, self.level * PLANE + p) for i, p in enumerate(self.places)
        ]

    def level_at(self, k):
        return lax.rem(self.level + self.depth - k, self.depth)

    def begin(self):
        @pl.loop(1, self.depth, unroll=self.depth <= 4)
        def _(k):
            self.level_copy(k).start()

        for c in self.spread(self.level):
            c.start()

    def forward(self):
        @pl.loop(1, self.depth, unroll=self.depth <= 4)
        def _(k):
            v = self.level_at(k)
            self.over(v * PLANE + self.place, 0, v, v, self.row).wait_recv()
            for c in self.spread(v):
                c.start()

    def arrive(self, v):
        for i, p in enumerate(self.places):
            self.over(v * PLANE + p, 1 + i, v, v, self.row).wait_recv()

    def finish(self):
        @pl.loop(1, self.depth, unroll=self.depth <= 4)
        def _(k):
            self.level_copy(k).wait_send()

        @pl.loop(0, self.depth)
        def _(v):
            for c in self.spread(v):
                c.wait_send()


def embed(
    nrows, nsnaps, slots,
    cols_hbm, count_hbm, tiles_hbm, x_hbm,
    left_ref, right_ref,
    cols_ref, count_ref, tiles_ref, out_tiles, in_tiles, x_all, parts, sums, s_all, image_ref,
    part0, pair0, mine0, chunks0, total0, part1, pair1, mine1, chunks1, total1,
    ready, local_sem, t_send, t_recv, p_send, p_recv, f_send, f_recv, c_send, c_recv,
    x_send0, x_recv0, x_send1, x_recv1, s_send0, s_recv0, s_send1, s_recv1, *total_sems,
):
    snap = lax.axis_index("tm")
    row = lax.axis_index("rows")
    piece = BLOCK // nsnaps
    depth = nrows // PLANE
    level = row // PLANE
    halves = range(COLS // BLOCK)

    def snap_peer(k):
        return lax.rem(snap + k, nsnaps)

    def row_peer(k):
        return lax.rem(row + k, nrows)

    barrier = pltpu.get_barrier_semaphore()

    side = row + 1 - 2 * lax.rem(row, 2)
    near = [side, level * PLANE + PLANE - 1 - lax.rem(side, PLANE)]
    near.append(level * PLANE + PLANE - 1 - lax.rem(row, PLANE))

    def greet(to):
        pl.semaphore_signal(barrier, inc=1, device_id=to, device_id_type=MESH)

    @pl.loop(1, depth)
    def _(k):
        greet((snap, row_peer(k * PLANE)))

    for r in near:
        greet((snap, r))
    for k in range(1, nsnaps):
        greet((snap_peer(k), row))

    x_in = [
        pltpu.make_async_copy(
            x_hbm.at[0, :, pl.ds(h * BLOCK, BLOCK)], x_all.at[h, row], local_sem.at[h]
        )
        for h in halves
    ]
    loads = [
        pltpu.make_async_copy(cols_hbm, cols_ref, local_sem.at[2]),
        pltpu.make_async_copy(count_hbm, count_ref, local_sem.at[3]),
        pltpu.make_async_copy(tiles_hbm.at[0], tiles_ref.at[pl.ds(0, slots)], local_sem.at[4]),
    ]
    for c in x_in + loads:
        c.start()
    tiles_ref[slots] = jnp.zeros((BLOCK, BLOCK), tiles_ref.dtype)
    for c in x_in:
        c.wait()

    spot = (snap, row, nrows)
    x_sems = ((x_send0, x_recv0), (x_send1, x_recv1))
    s_sems = ((s_send0, s_recv0), (s_send1, s_recv1))
    x_relay = [Relay(lambda b, h=h: x_all.at[h, b], *x_sems[h], spot) for h in halves]
    s_relay = [Relay(lambda b, h=h: s_all.at[h, snap, b], *s_sems[h], spot) for h in halves]

    pl.semaphore_wait(barrier, depth - 1 + len(near) + nsnaps - 1)
    for r in x_relay:
        r.begin()
    for r in near:
        pl.semaphore_signal(ready, inc=1, device_id=(snap, r), device_id_type=MESH)

    for c in loads:
        c.wait()
    live = [jnp.where(s < count_ref[0, 0], cols_ref[0, s], -1) for s in range(slots)]

    @pl.loop(0, nrows)
    def _(c):
        slot = jnp.int32(slots)
        for s in range(slots):
            slot = jnp.where(live[s] == c, s, slot)
        out_tiles[c] = tiles_ref[slot]

    in_tiles[row] = out_tiles[row]

    def t_copy(src, k):
        to = row_peer(k)
        return remote(
            out_tiles.at[to], in_tiles.at[src], t_send.at[k], t_recv.at[src], (snap, to)
        )

    pl.semaphore_wait(ready, len(near))

    @pl.loop(1, nrows, unroll=nrows <= 16)
    def _(k):
        t_copy(row, k).start()

    x_relay[0].forward()

    x_relay[1].forward()

    def p_copy(h, src, to, k):
        view = parts.at[h, src, to]
        return remote(view, view, p_send.at[h, k], p_recv.at[h, src], (to, row))

    def f_copy(h, src, to, k):
        view = sums.at[h, src]
        return remote(view, view, f_send.at[h, k], f_recv.at[h, src], (to, row))

    for h in halves:
        value = None
        for k in range(depth):
            v = lax.rem(level + depth - k, depth)
            x_relay[h].arrive(v)
            first = v * PLANE
            tiles_of = jnp.concatenate([out_tiles[first + i] for i in range(PLANE)], axis=1)
            term = dot_nn(tiles_of, x_all[h, pl.ds(first, PLANE)].reshape(PLANE * BLOCK, BLOCK))
            value = term if value is None else value + term
        parts[h, snap] = value.reshape(nsnaps, piece, BLOCK)
        for k in range(1, nsnaps):
            p_copy(h, snap, snap_peer(k), k).start()
        for k in range(1, nsnaps):
            p_copy(h, snap_peer(k), snap, k).wait_recv()
        summed = parts[h, 0, snap]
        for k in range(1, nsnaps):
            summed = summed + parts[h, k, snap]
        sums[h, snap] = summed
        s_all[h, snap, row] = summed.astype(jnp.bfloat16)
        s_relay[h].begin()

    for h in halves:
        s_relay[h].forward()

    def c_copy(h, src, v, to, k):
        view = s_all.at[h, src, pl.ds(v * PLANE, PLANE)]
        return remote(view, view, c_send.at[h, k, v], c_recv.at[h, src, v], (to, row))

    def share(h):
        @pl.loop(0, depth)
        def _(k):
            v = lax.rem(level + depth - k, depth)
            s_relay[h].arrive(v)
            for i in range(1, nsnaps):
                c_copy(h, snap, v, snap_peer(i), i).start()

    def shared(h):
        @pl.loop(0, depth)
        def _(v):
            for i in range(1, nsnaps):
                c_copy(h, snap_peer(i), v, snap, i).wait_recv()

    def s_of(h, t):
        return s_all[h, t].reshape(nrows * piece, BLOCK)

    def tiles_at(t):
        return in_tiles[:, t * piece : (t + 1) * piece, :].reshape(nrows * piece, BLOCK)

    def image_of(h):
        return functools.reduce(
            jnp.add, [dot_tn(tiles_at(t), s_of(h, t)) for t in range(nsnaps)]
        )

    def gram_of(g, h):
        return functools.reduce(jnp.add, [dot_tn(s_of(g, t), s_of(h, t)) for t in range(nsnaps)])

    where = (snap, row, nsnaps, nrows)
    first_total = Total((part0, pair0, mine0, chunks0, total0), total_sems[:8], where)
    other_total = Total((part1, pair1, mine1, chunks1, total1), total_sems[8:], where)
    lo, hi = slice(0, BLOCK), slice(BLOCK, COLS)

    share(0)

    @pl.loop(1, nrows, unroll=nrows <= 16)
    def _(k):
        t_copy(row_peer(nrows - k), k).wait_recv()

    shared(0)
    image = image_of(0)
    image_ref[0] = image
    part0[...] = dot_tn(image, image, HIGHEST)
    first_total.pairs()

    share(1)
    first_total.scatter()
    shared(1)
    image = image_of(1)
    image_ref[1] = image
    part1[lo, :] = dot_tn(image, image_ref[0], HIGHEST)
    part1[hi, :] = dot_tn(image, image, HIGHEST)
    other_total.pairs()

    for h in halves:
        for k in range(1, nsnaps):
            f_copy(h, snap, snap_peer(k), k).start()
    gram00, gram10, gram11 = gram_of(0, 0), gram_of(1, 0), gram_of(1, 1)
    other_total.scatter()
    first_total.reduce()

    upper = Elimination(gram00).run().result()
    other_total.reduce()
    for h in halves:
        for k in range(1, nsnaps):
            f_copy(h, snap_peer(k), snap, k).wait_recv()
    left_lo, left_hi = (sums[h].reshape(BLOCK, BLOCK) for h in halves)
    below = dot_nt(gram10, upper)
    left_head = dot_nt(left_lo, upper)
    left_tail = left_hi - dot_nt(left_head, below)
    left_lower = Elimination(gram11 - dot_nt(below, below)).run(4)
    left_scale = math.sqrt(nrows * BLOCK)
    left_ref[:, lo] = left_head * left_scale

    first_total.share()
    first_total.arrive()
    upper = Elimination(total0[...]).run().result()
    other_total.share()
    head = dot_nt(image_ref[0], upper)
    scale = math.sqrt(nsnaps * nrows * BLOCK)
    right_ref[:, lo] = head * scale
    other_total.arrive()
    below = dot_nt(total1[lo, :], upper)
    lower = Elimination(total1[hi, :] - dot_nt(below, below)).run().result()
    tail = image_ref[1] - dot_nt(head, below)
    right_ref[:, hi] = dot_nt(tail, lower) * scale
    left_ref[:, hi] = dot_nt(left_tail, left_lower.run(4).result()) * left_scale

    for r in x_relay + s_relay:
        r.finish()
    first_total.finish()
    other_total.finish()
    for h in halves:
        for k in range(1, nsnaps):
            p_copy(h, snap, snap_peer(k), k).wait_send()
            f_copy(h, snap, snap_peer(k), k).wait_send()

            @pl.loop(0, depth)
            def _(v):
                c_copy(h, snap, v, snap_peer(k), k).wait_send()

    @pl.loop(1, nrows, unroll=nrows <= 16)
    def _(k):
        t_copy(row, k).wait_send()


def hand_over(left_in, right_in, left_out, right_out):
    left_out[...] = left_in[...]
    right_out[...] = right_in[...]


def on_device(tiles, tile_cols, tile_count, start_right):
    nrows = lax.axis_size("rows")
    nsnaps = lax.axis_size("tm")
    slots = tiles.shape[1]
    depth = nrows // PLANE
    piece = BLOCK // nsnaps
    f32, bf16 = jnp.float32, jnp.bfloat16
    vmem = pl.BlockSpec(memory_space=pltpu.VMEM)
    hbm = pl.BlockSpec(memory_space=pltpu.HBM)
    dma = lambda *n: pltpu.SemaphoreType.DMA(n)
    block = jax.ShapeDtypeStruct((BLOCK, COLS), f32)
    params = dict(vmem_limit_bytes=60 * 1024 * 1024)
    totals, total_sems = [], []
    for size in (BLOCK, 2 * BLOCK):
        half = size // nsnaps
        owners = min(nrows, half // 8)
        totals += [
            pltpu.VMEM((size, BLOCK), f32),
            pltpu.VMEM((nsnaps, half, BLOCK), f32),
            pltpu.VMEM((half, BLOCK), f32),
            pltpu.VMEM((nrows, half // owners, BLOCK), f32),
            pltpu.VMEM((size, BLOCK), f32),
        ]
        total_sems += [dma(nsnaps), dma(nsnaps)] + [dma(nrows)] * 4 + [dma(nsnaps), dma(nsnaps)]
    left, right = pl.pallas_call(
        functools.partial(embed, nrows, nsnaps, slots),
        out_shape=(block, block),
        in_specs=[hbm] * 4,
        out_specs=(vmem, vmem),
        scratch_shapes=[
            pltpu.SMEM(tile_cols.shape, jnp.int32),
            pltpu.SMEM(tile_count.shape, jnp.int32),
            pltpu.VMEM((slots + 1, BLOCK, BLOCK), bf16),
            pltpu.VMEM((nrows, BLOCK, BLOCK), bf16),
            pltpu.VMEM((nrows, BLOCK, BLOCK), bf16),
            pltpu.VMEM((2, nrows, BLOCK, BLOCK), bf16),
            pltpu.VMEM((2, nsnaps, nsnaps, piece, BLOCK), f32),
            pltpu.VMEM((2, nsnaps, piece, BLOCK), f32),
            pltpu.VMEM((2, nsnaps, nrows, piece, BLOCK), bf16),
            pltpu.VMEM((2, BLOCK, BLOCK), f32),
            *totals,
            pltpu.SemaphoreType.REGULAR,
            dma(5), dma(nrows), dma(nrows),
            *[dma(2, nsnaps)] * 4,
            *[dma(2, nsnaps, depth)] * 2,
            *[dma(4, depth)] * 8,
            *total_sems,
        ],
        compiler_params=pltpu.CompilerParams(collective_id=0, has_side_effects=True, **params),
        name="embed",
    )(tile_cols, tile_count, tiles, start_right)
    left, right = pl.pallas_call(
        hand_over,
        out_shape=(block, block),
        in_specs=[vmem, vmem],
        out_specs=(vmem, vmem),
        compiler_params=pltpu.CompilerParams(**params),
        name="hand_over",
    )(left, right)
    return (left, right[None])


def solution(mesh):
    placed = (P("tm", "rows", None, None), P("tm", "rows"), P("tm", "rows"), P("tm", "rows", None))
    return jax.shard_map(
        on_device,
        mesh=mesh,
        in_specs=placed,
        out_specs=(P("rows", None), P("tm", "rows", None)),
        check_vma=False,
    )
```

```python
import functools
import math

import jax
import jax.numpy as jnp
from jax import lax
from jax.experimental import pallas as pl
from jax.experimental.pallas import tpu as pltpu
from jax.sharding import PartitionSpec as P

BLOCK = 128
COLS = 256
PLANE = 4
WIDE = 16
MESH = pl.DeviceIdType.MESH
HIGHEST = lax.Precision.HIGHEST


def dot_nn(a, b):
    return jnp.dot(a, b, preferred_element_type=jnp.float32)


def dot_tn(a, b, precision=None):
    return lax.dot_general(
        a, b, (((0,), (0,)), ((), ())), precision=precision, preferred_element_type=jnp.float32
    )


def dot_nt(a, b):
    return lax.dot_general(
        a, b, (((1,), (1,)), ((), ())), precision=HIGHEST, preferred_element_type=jnp.float32
    )


def remote(src, dst, send, recv, to):
    return pltpu.make_async_remote_copy(
        src_ref=src, dst_ref=dst, send_sem=send, recv_sem=recv, device_id=to, device_id_type=MESH
    )


class Elimination:
    def __init__(self, matrix):
        self.z = [matrix[8 * g : 8 * g + 8, :] for g in range(BLOCK // 8)]
        self.at = 0

    def run(self, steps=BLOCK // WIDE):
        lane = lax.broadcasted_iota(jnp.int32, (8, BLOCK), 1)
        sub = lax.broadcasted_iota(jnp.int32, (8, BLOCK), 0)
        across = lambda v, j: jnp.broadcast_to(v[:, j : j + 1], (8, BLOCK))
        down = lambda v, i: jnp.broadcast_to(v[i : i + 1, :], (8, BLOCK))
        z, halves = self.z, range(WIDE // 8)
        for _ in range(steps):
            g0 = self.at
            self.at += WIDE // 8
            j0 = 8 * g0
            inside = jnp.logical_and(lane >= j0, lane < j0 + WIDE)
            panel = [[across(z[g0 + s], j0 + q) for s in halves] for q in range(WIDE)]
            both = [
                jnp.where(inside, jnp.where(lane == sub + (j0 + 8 * s), 1.0, 0.0), z[g0 + s])
                for s in halves
            ]
            kept = list(both)
            inverse = [jnp.zeros((8, BLOCK), jnp.float32) for s in halves]
            for p in range(WIDE):
                ps, pi = p // 8, p % 8
                here = sub == pi
                recip = 1.0 / down(panel[p][ps], pi)
                inverse[ps] = jnp.where(here, recip, inverse[ps])
                column = list(panel[p])
                column[ps] = jnp.where(here, 0.0, column[ps])
                factor = [c * recip for c in column]
                for q in range(p + 1, WIDE):
                    d = down(panel[q][ps], pi)
                    for s in halves:
                        step = (column[s] * d) * recip if q == p + 1 else factor[s] * d
                        panel[q][s] = panel[q][s] - step
                pivot_row = down(both[ps], pi)
                kept[ps] = jnp.where(here, pivot_row, kept[ps])
                for s in halves:
                    both[s] = both[s] - factor[s] * pivot_row
            rows = [down(both[q // 8] * inverse[q // 8], q % 8) for q in range(WIDE)]
            for s in halves:
                z[g0 + s] = kept[s] * jnp.sqrt(inverse[s])
            for g in range(g0 + WIDE // 8, BLOCK // 8):
                new = jnp.where(inside, 0.0, z[g])
                for q in range(WIDE):
                    new = new - across(z[g], j0 + q) * rows[q]
                z[g] = new
        return self

    def result(self):
        lane = lax.broadcasted_iota(jnp.int32, (8, BLOCK), 1)
        sub = lax.broadcasted_iota(jnp.int32, (8, BLOCK), 0)
        return jnp.concatenate(
            [jnp.where(lane <= sub + 8 * g, z, 0.0) for g, z in enumerate(self.z)], axis=0
        )


class Total:
    def __init__(self, refs, sems, place):
        self.part, self.pair, self.mine, self.chunks, self.result = refs
        self.hs, self.hr, self.gs, self.gr, self.rs, self.rr, self.bs, self.br = sems
        self.snap, self.row, self.nsnaps, self.nrows = place
        self.half = self.part.shape[0] // self.nsnaps
        self.chunk = self.chunks.shape[1]
        self.owners = self.half // self.chunk
        self.first = (self.nrows - self.owners) // 2

    def snap_peer(self, k):
        return lax.rem(self.snap + k, self.nsnaps)

    def h_copy(self, src, to, k):
        at = pl.ds(pl.multiple_of(to * self.half, self.half), self.half)
        return remote(
            self.part.at[at], self.pair.at[src], self.hs.at[k], self.hr.at[src], (to, self.row)
        )

    def g_copy(self, src, owner):
        at = pl.ds(pl.multiple_of(owner * self.chunk, self.chunk), self.chunk)
        return remote(
            self.mine.at[at], self.chunks.at[src], self.gs.at[owner], self.gr.at[src],
            (self.snap, self.first + owner),
        )

    def r_copy(self, owner, to):
        at = pl.multiple_of(self.snap * self.half + owner * self.chunk, self.chunk)
        view = self.result.at[pl.ds(at, self.chunk)]
        return remote(view, view, self.rs.at[to], self.rr.at[owner], (self.snap, to))

    def b_copy(self, src, to, k):
        view = self.result.at[pl.ds(pl.multiple_of(src * self.half, self.half), self.half)]
        return remote(view, view, self.bs.at[k], self.br.at[src], (to, self.row))

    def if_owner(self, body):
        if self.owners == self.nrows:
            body()
        else:
            mine = jnp.logical_and(self.row >= self.first, self.row < self.first + self.owners)
            pl.when(mine)(body)

    def each_owner(self, body):
        @pl.loop(0, self.owners, unroll=self.nrows <= 16)
        def _(o):
            owner = lax.rem(o + self.row, self.owners)
            pl.when(self.first + owner != self.row)(lambda: body(owner))

    def pairs(self):
        for k in range(1, self.nsnaps):
            self.h_copy(self.snap, self.snap_peer(k), k).start()

    def scatter(self):
        for k in range(1, self.nsnaps):
            self.h_copy(self.snap_peer(k), self.snap, k).wait_recv()
        at = pl.ds(pl.multiple_of(self.snap * self.half, self.half), self.half)
        mine = self.part[at, :]
        for k in range(1, self.nsnaps):
            mine = mine + self.pair[self.snap_peer(k)]
        self.mine[...] = mine
        self.each_owner(lambda owner: self.g_copy(self.row, owner).start())

    def reduce(self):
        def body():
            owner = self.row - self.first
            at = pl.ds(pl.multiple_of(owner * self.chunk, self.chunk), self.chunk)

            def step(k, acc):
                src = lax.rem(self.row + self.nrows - k, self.nrows)
                self.g_copy(src, owner).wait_recv()
                return acc + self.chunks[src]

            acc = lax.fori_loop(1, self.nrows, step, self.mine[at, :], unroll=self.nrows <= 16)
            at = pl.multiple_of(self.snap * self.half + owner * self.chunk, self.chunk)
            self.result[pl.ds(at, self.chunk), :] = acc

            @pl.loop(1, self.nrows, unroll=self.nrows <= 16)
            def _(k):
                self.r_copy(owner, lax.rem(self.row + k, self.nrows)).start()

        self.if_owner(body)

    def share(self):
        self.each_owner(lambda owner: self.r_copy(owner, self.row).wait_recv())
        for k in range(1, self.nsnaps):
            self.b_copy(self.snap, self.snap_peer(k), k).start()

    def arrive(self):
        for k in range(1, self.nsnaps):
            self.b_copy(self.snap_peer(k), self.snap, k).wait_recv()

    def finish(self):
        for k in range(1, self.nsnaps):
            self.h_copy(self.snap, self.snap_peer(k), k).wait_send()
            self.b_copy(self.snap, self.snap_peer(k), k).wait_send()
        self.each_owner(lambda owner: self.g_copy(self.row, owner).wait_send())

        def body():
            @pl.loop(1, self.nrows, unroll=self.nrows <= 16)
            def _(k):
                self.r_copy(self.row - self.first, lax.rem(self.row + k, self.nrows)).wait_send()

        self.if_owner(body)


class Relay:
    def __init__(self, view, send, recv, place):
        self.view, self.send, self.recv = view, send, recv
        self.snap, self.row, self.nrows = place
        self.depth = self.nrows // PLANE
        self.level, self.place = self.row // PLANE, lax.rem(self.row, PLANE)
        side = self.place + 1 - 2 * lax.rem(self.place, 2)
        self.places = (side, PLANE - 1 - side, PLANE - 1 - self.place)

    def over(self, b, kind, at, slot, to):
        view = self.view(b)
        return remote(view, view, self.send.at[kind, slot], self.recv.at[kind, at], (self.snap, to))

    def level_copy(self, k):
        to = lax.rem(self.level + k, self.depth)
        return self.over(self.row, 0, self.level, to, to * PLANE + self.place)

    def spread(self, v):
        b = v * PLANE + self.place
        return [
            self.over(b, 1 + i, v, v, self.level * PLANE + p) for i, p in enumerate(self.places)
        ]

    def level_at(self, k):
        return lax.rem(self.level + self.depth - k, self.depth)

    def begin(self):
        @pl.loop(1, self.depth, unroll=self.depth <= 4)
        def _(k):
            self.level_copy(k).start()

        for c in self.spread(self.level):
            c.start()

    def forward(self):
        @pl.loop(1, self.depth, unroll=self.depth <= 4)
        def _(k):
            v = self.level_at(k)
            self.over(v * PLANE + self.place, 0, v, v, self.row).wait_recv()
            for c in self.spread(v):
                c.start()

    def arrive(self, v):
        for i, p in enumerate(self.places):
            self.over(v * PLANE + p, 1 + i, v, v, self.row).wait_recv()

    def finish(self):
        @pl.loop(1, self.depth, unroll=self.depth <= 4)
        def _(k):
            self.level_copy(k).wait_send()

        @pl.loop(0, self.depth)
        def _(v):
            for c in self.spread(v):
                c.wait_send()


def embed(
    nrows, nsnaps, slots,
    cols_hbm, count_hbm, tiles_hbm, x_hbm,
    left_ref, right_ref,
    cols_ref, count_ref, tiles_ref, out_tiles, in_tiles, x_all, parts, sums, s_all, image_ref,
    part0, pair0, mine0, chunks0, total0, part1, pair1, mine1, chunks1, total1,
    ready, local_sem, t_send, t_recv, p_send, p_recv, f_send, f_recv, c_send, c_recv,
    x_send0, x_recv0, x_send1, x_recv1, s_send0, s_recv0, s_send1, s_recv1, *total_sems,
):
    snap = lax.axis_index("tm")
    row = lax.axis_index("rows")
    piece = BLOCK // nsnaps
    depth = nrows // PLANE
    level = row // PLANE
    halves = range(COLS // BLOCK)

    def snap_peer(k):
        return lax.rem(snap + k, nsnaps)

    def row_peer(k):
        return lax.rem(row + k, nrows)

    barrier = pltpu.get_barrier_semaphore()

    side = row + 1 - 2 * lax.rem(row, 2)
    near = [side, level * PLANE + PLANE - 1 - lax.rem(side, PLANE)]
    near.append(level * PLANE + PLANE - 1 - lax.rem(row, PLANE))

    def greet(to):
        pl.semaphore_signal(barrier, inc=1, device_id=to, device_id_type=MESH)

    @pl.loop(1, depth)
    def _(k):
        greet((snap, row_peer(k * PLANE)))

    for r in near:
        greet((snap, r))
    for k in range(1, nsnaps):
        greet((snap_peer(k), row))

    x_in = [
        pltpu.make_async_copy(
            x_hbm.at[0, :, pl.ds(h * BLOCK, BLOCK)], x_all.at[h, row], local_sem.at[h]
        )
        for h in halves
    ]
    loads = [
        pltpu.make_async_copy(cols_hbm, cols_ref, local_sem.at[2]),
        pltpu.make_async_copy(count_hbm, count_ref, local_sem.at[3]),
        pltpu.make_async_copy(tiles_hbm.at[0], tiles_ref.at[pl.ds(0, slots)], local_sem.at[4]),
    ]
    for c in x_in + loads:
        c.start()
    tiles_ref[slots] = jnp.zeros((BLOCK, BLOCK), tiles_ref.dtype)
    for c in x_in:
        c.wait()

    spot = (snap, row, nrows)
    x_sems = ((x_send0, x_recv0), (x_send1, x_recv1))
    s_sems = ((s_send0, s_recv0), (s_send1, s_recv1))
    x_relay = [Relay(lambda b, h=h: x_all.at[h, b], *x_sems[h], spot) for h in halves]
    s_relay = [Relay(lambda b, h=h: s_all.at[h, snap, b], *s_sems[h], spot) for h in halves]

    pl.semaphore_wait(barrier, depth - 1 + len(near) + nsnaps - 1)
    for r in x_relay:
        r.begin()
    for r in near:
        pl.semaphore_signal(ready, inc=1, device_id=(snap, r), device_id_type=MESH)

    for c in loads:
        c.wait()
    live = [jnp.where(s < count_ref[0, 0], cols_ref[0, s], -1) for s in range(slots)]

    @pl.loop(0, nrows)
    def _(c):
        slot = jnp.int32(slots)
        for s in range(slots):
            slot = jnp.where(live[s] == c, s, slot)
        out_tiles[c] = tiles_ref[slot]

    in_tiles[row] = out_tiles[row]

    def t_copy(src, k):
        to = row_peer(k)
        return remote(
            out_tiles.at[to], in_tiles.at[src], t_send.at[k], t_recv.at[src], (snap, to)
        )

    pl.semaphore_wait(ready, len(near))

    @pl.loop(1, nrows, unroll=nrows <= 16)
    def _(k):
        t_copy(row, k).start()

    x_relay[0].forward()

    x_relay[1].forward()

    def p_copy(h, src, to, k):
        view = parts.at[h, src, to]
        return remote(view, view, p_send.at[h, k], p_recv.at[h, src], (to, row))

    def f_copy(h, src, to, k):
        view = sums.at[h, src]
        return remote(view, view, f_send.at[h, k], f_recv.at[h, src], (to, row))

    for h in halves:
        value = None
        for k in range(depth):
            v = lax.rem(level + depth - k, depth)
            x_relay[h].arrive(v)
            first = v * PLANE
            tiles_of = jnp.concatenate([out_tiles[first + i] for i in range(PLANE)], axis=1)
            term = dot_nn(tiles_of, x_all[h, pl.ds(first, PLANE)].reshape(PLANE * BLOCK, BLOCK))
            value = term if value is None else value + term
        parts[h, snap] = value.reshape(nsnaps, piece, BLOCK)
        for k in range(1, nsnaps):
            p_copy(h, snap, snap_peer(k), k).start()
        for k in range(1, nsnaps):
            p_copy(h, snap_peer(k), snap, k).wait_recv()
        summed = parts[h, 0, snap]
        for k in range(1, nsnaps):
            summed = summed + parts[h, k, snap]
        sums[h, snap] = summed
        s_all[h, snap, row] = summed.astype(jnp.bfloat16)
        s_relay[h].begin()

    for h in halves:
        s_relay[h].forward()

    def c_copy(h, src, v, to, k):
        view = s_all.at[h, src, pl.ds(v * PLANE, PLANE)]
        return remote(view, view, c_send.at[h, k, v], c_recv.at[h, src, v], (to, row))

    def share(h):
        @pl.loop(0, depth)
        def _(k):
            v = lax.rem(level + depth - k, depth)
            s_relay[h].arrive(v)
            for i in range(1, nsnaps):
                c_copy(h, snap, v, snap_peer(i), i).start()

    def shared(h):
        @pl.loop(0, depth)
        def _(v):
            for i in range(1, nsnaps):
                c_copy(h, snap_peer(i), v, snap, i).wait_recv()

    def s_of(h, t):
        return s_all[h, t].reshape(nrows * piece, BLOCK)

    def tiles_at(t):
        return in_tiles[:, t * piece : (t + 1) * piece, :].reshape(nrows * piece, BLOCK)

    def image_of(h):
        return functools.reduce(
            jnp.add, [dot_tn(tiles_at(t), s_of(h, t)) for t in range(nsnaps)]
        )

    def gram_of(g, h):
        return functools.reduce(jnp.add, [dot_tn(s_of(g, t), s_of(h, t)) for t in range(nsnaps)])

    where = (snap, row, nsnaps, nrows)
    first_total = Total((part0, pair0, mine0, chunks0, total0), total_sems[:8], where)
    other_total = Total((part1, pair1, mine1, chunks1, total1), total_sems[8:], where)
    lo, hi = slice(0, BLOCK), slice(BLOCK, COLS)

    share(0)

    @pl.loop(1, nrows, unroll=nrows <= 16)
    def _(k):
        t_copy(row_peer(nrows - k), k).wait_recv()

    shared(0)
    image = image_of(0)
    image_ref[0] = image
    part0[...] = dot_tn(image, image, HIGHEST)
    first_total.pairs()

    share(1)
    first_total.scatter()
    shared(1)
    image = image_of(1)
    image_ref[1] = image
    part1[lo, :] = dot_tn(image, image_ref[0], HIGHEST)
    part1[hi, :] = dot_tn(image, image, HIGHEST)
    other_total.pairs()

    for h in halves:
        for k in range(1, nsnaps):
            f_copy(h, snap, snap_peer(k), k).start()
    gram00, gram10, gram11 = gram_of(0, 0), gram_of(1, 0), gram_of(1, 1)
    other_total.scatter()
    first_total.reduce()

    upper = Elimination(gram00).run(6)
    other_total.reduce()
    upper = upper.run(8 - 6).result()
    for h in halves:
        for k in range(1, nsnaps):
            f_copy(h, snap_peer(k), snap, k).wait_recv()
    left_lo, left_hi = (sums[h].reshape(BLOCK, BLOCK) for h in halves)
    below = dot_nt(gram10, upper)
    left_head = dot_nt(left_lo, upper)
    left_tail = left_hi - dot_nt(left_head, below)
    left_lower = Elimination(gram11 - dot_nt(below, below)).run(6)
    left_scale = math.sqrt(nrows * BLOCK)
    left_ref[:, lo] = left_head * left_scale

    first_total.share()
    first_total.arrive()
    upper = Elimination(total0[...]).run(6)
    other_total.share()
    upper = upper.run(8 - 6).result()
    head = dot_nt(image_ref[0], upper)
    scale = math.sqrt(nsnaps * nrows * BLOCK)
    right_ref[:, lo] = head * scale
    other_total.arrive()
    below = dot_nt(total1[lo, :], upper)
    lower = Elimination(total1[hi, :] - dot_nt(below, below)).run().result()
    tail = image_ref[1] - dot_nt(head, below)
    right_ref[:, hi] = dot_nt(tail, lower) * scale
    left_ref[:, hi] = dot_nt(left_tail, left_lower.run(8 - 6).result()) * left_scale

    for r in x_relay + s_relay:
        r.finish()
    first_total.finish()
    other_total.finish()
    for h in halves:
        for k in range(1, nsnaps):
            p_copy(h, snap, snap_peer(k), k).wait_send()
            f_copy(h, snap, snap_peer(k), k).wait_send()

            @pl.loop(0, depth)
            def _(v):
                c_copy(h, snap, v, snap_peer(k), k).wait_send()

    @pl.loop(1, nrows, unroll=nrows <= 16)
    def _(k):
        t_copy(row, k).wait_send()


def hand_over(left_in, right_in, left_out, right_out):
    left_out[...] = left_in[...]
    right_out[...] = right_in[...]


def on_device(tiles, tile_cols, tile_count, start_right):
    nrows = lax.axis_size("rows")
    nsnaps = lax.axis_size("tm")
    slots = tiles.shape[1]
    depth = nrows // PLANE
    piece = BLOCK // nsnaps
    f32, bf16 = jnp.float32, jnp.bfloat16
    vmem = pl.BlockSpec(memory_space=pltpu.VMEM)
    hbm = pl.BlockSpec(memory_space=pltpu.HBM)
    dma = lambda *n: pltpu.SemaphoreType.DMA(n)
    block = jax.ShapeDtypeStruct((BLOCK, COLS), f32)
    params = dict(vmem_limit_bytes=60 * 1024 * 1024)
    totals, total_sems = [], []
    for size in (BLOCK, 2 * BLOCK):
        half = size // nsnaps
        owners = min(nrows, half // (8 if size == BLOCK else 16))
        totals += [
            pltpu.VMEM((size, BLOCK), f32),
            pltpu.VMEM((nsnaps, half, BLOCK), f32),
            pltpu.VMEM((half, BLOCK), f32),
            pltpu.VMEM((nrows, half // owners, BLOCK), f32),
            pltpu.VMEM((size, BLOCK), f32),
        ]
        total_sems += [dma(nsnaps), dma(nsnaps)] + [dma(nrows)] * 4 + [dma(nsnaps), dma(nsnaps)]
    left, right = pl.pallas_call(
        functools.partial(embed, nrows, nsnaps, slots),
        out_shape=(block, block),
        in_specs=[hbm] * 4,
        out_specs=(vmem, vmem),
        scratch_shapes=[
            pltpu.SMEM(tile_cols.shape, jnp.int32),
            pltpu.SMEM(tile_count.shape, jnp.int32),
            pltpu.VMEM((slots + 1, BLOCK, BLOCK), bf16),
            pltpu.VMEM((nrows, BLOCK, BLOCK), bf16),
            pltpu.VMEM((nrows, BLOCK, BLOCK), bf16),
            pltpu.VMEM((2, nrows, BLOCK, BLOCK), bf16),
            pltpu.VMEM((2, nsnaps, nsnaps, piece, BLOCK), f32),
            pltpu.VMEM((2, nsnaps, piece, BLOCK), f32),
            pltpu.VMEM((2, nsnaps, nrows, piece, BLOCK), bf16),
            pltpu.VMEM((2, BLOCK, BLOCK), f32),
            *totals,
            pltpu.SemaphoreType.REGULAR,
            dma(5), dma(nrows), dma(nrows),
            *[dma(2, nsnaps)] * 4,
            *[dma(2, nsnaps, depth)] * 2,
            *[dma(4, depth)] * 8,
            *total_sems,
        ],
        compiler_params=pltpu.CompilerParams(collective_id=0, has_side_effects=True, **params),
        name="embed",
    )(tile_cols, tile_count, tiles, start_right)
    left, right = pl.pallas_call(
        hand_over,
        out_shape=(block, block),
        in_specs=[vmem, vmem],
        out_specs=(vmem, vmem),
        compiler_params=pltpu.CompilerParams(**params),
        name="hand_over",
    )(left, right)
    return (left, right[None])


def solution(mesh):
    placed = (P("tm", "rows", None, None), P("tm", "rows"), P("tm", "rows"), P("tm", "rows", None))
    return jax.shard_map(
        on_device,
        mesh=mesh,
        in_specs=placed,
        out_specs=(P("rows", None), P("tm", "rows", None)),
        check_vma=False,
    )
```

```python
import functools
import math

import jax
import jax.numpy as jnp
from jax import lax
from jax.experimental import pallas as pl
from jax.experimental.pallas import tpu as pltpu
from jax.sharding import PartitionSpec as P

BLOCK = 128
COLS = 256
PLANE = 4
WIDE = 16
MESH = pl.DeviceIdType.MESH
HIGHEST = lax.Precision.HIGHEST


def dot_nn(a, b):
    return jnp.dot(a, b, preferred_element_type=jnp.float32)


def dot_tn(a, b, precision=None):
    return lax.dot_general(
        a, b, (((0,), (0,)), ((), ())), precision=precision, preferred_element_type=jnp.float32
    )


def dot_nt(a, b):
    return lax.dot_general(
        a, b, (((1,), (1,)), ((), ())), precision=HIGHEST, preferred_element_type=jnp.float32
    )


def remote(src, dst, send, recv, to):
    return pltpu.make_async_remote_copy(
        src_ref=src, dst_ref=dst, send_sem=send, recv_sem=recv, device_id=to, device_id_type=MESH
    )


class Elimination:
    def __init__(self, matrix):
        self.z = [matrix[8 * g : 8 * g + 8, :] for g in range(BLOCK // 8)]
        self.at = 0

    def run(self, steps=BLOCK // WIDE):
        lane = lax.broadcasted_iota(jnp.int32, (8, BLOCK), 1)
        sub = lax.broadcasted_iota(jnp.int32, (8, BLOCK), 0)
        across = lambda v, j: jnp.broadcast_to(v[:, j : j + 1], (8, BLOCK))
        down = lambda v, i: jnp.broadcast_to(v[i : i + 1, :], (8, BLOCK))
        z, halves = self.z, range(WIDE // 8)
        for _ in range(steps):
            g0 = self.at
            self.at += WIDE // 8
            j0 = 8 * g0
            inside = jnp.logical_and(lane >= j0, lane < j0 + WIDE)
            panel = [[across(z[g0 + s], j0 + q) for s in halves] for q in range(WIDE)]
            both = [
                jnp.where(inside, jnp.where(lane == sub + (j0 + 8 * s), 1.0, 0.0), z[g0 + s])
                for s in halves
            ]
            kept = list(both)
            inverse = [jnp.zeros((8, BLOCK), jnp.float32) for s in halves]
            for p in range(WIDE):
                ps, pi = p // 8, p % 8
                here = sub == pi
                recip = 1.0 / down(panel[p][ps], pi)
                inverse[ps] = jnp.where(here, recip, inverse[ps])
                column = list(panel[p])
                column[ps] = jnp.where(here, 0.0, column[ps])
                factor = [c * recip for c in column]
                for q in range(p + 1, WIDE):
                    d = down(panel[q][ps], pi)
                    for s in halves:
                        step = (column[s] * d) * recip if q == p + 1 else factor[s] * d
                        panel[q][s] = panel[q][s] - step
                pivot_row = down(both[ps], pi)
                kept[ps] = jnp.where(here, pivot_row, kept[ps])
                for s in halves:
                    both[s] = both[s] - factor[s] * pivot_row
            rows = [down(both[q // 8] * inverse[q // 8], q % 8) for q in range(WIDE)]
            for s in halves:
                z[g0 + s] = kept[s] * jnp.sqrt(inverse[s])
            for g in range(g0 + WIDE // 8, BLOCK // 8):
                new = jnp.where(inside, 0.0, z[g])
                for q in range(WIDE):
                    new = new - across(z[g], j0 + q) * rows[q]
                z[g] = new
        return self

    def result(self):
        lane = lax.broadcasted_iota(jnp.int32, (8, BLOCK), 1)
        sub = lax.broadcasted_iota(jnp.int32, (8, BLOCK), 0)
        return jnp.concatenate(
            [jnp.where(lane <= sub + 8 * g, z, 0.0) for g, z in enumerate(self.z)], axis=0
        )


class Total:
    def __init__(self, refs, sems, place):
        self.part, self.pair, self.mine, self.chunks, self.result = refs
        self.hs, self.hr, self.gs, self.gr, self.rs, self.rr, self.bs, self.br = sems
        self.snap, self.row, self.nsnaps, self.nrows = place
        self.half = self.part.shape[0] // self.nsnaps
        self.chunk = self.chunks.shape[1]
        self.owners = self.half // self.chunk
        self.first = (self.nrows - self.owners) // 2

    def snap_peer(self, k):
        return lax.rem(self.snap + k, self.nsnaps)

    def h_copy(self, src, to, k):
        at = pl.ds(pl.multiple_of(to * self.half, self.half), self.half)
        return remote(
            self.part.at[at], self.pair.at[src], self.hs.at[k], self.hr.at[src], (to, self.row)
        )

    def g_copy(self, src, owner):
        at = pl.ds(pl.multiple_of(owner * self.chunk, self.chunk), self.chunk)
        return remote(
            self.mine.at[at], self.chunks.at[src], self.gs.at[owner], self.gr.at[src],
            (self.snap, self.first + owner),
        )

    def r_copy(self, owner, to):
        at = pl.multiple_of(self.snap * self.half + owner * self.chunk, self.chunk)
        view = self.result.at[pl.ds(at, self.chunk)]
        return remote(view, view, self.rs.at[to], self.rr.at[owner], (self.snap, to))

    def b_copy(self, src, to, k):
        view = self.result.at[pl.ds(pl.multiple_of(src * self.half, self.half), self.half)]
        return remote(view, view, self.bs.at[k], self.br.at[src], (to, self.row))

    def if_owner(self, body):
        if self.owners == self.nrows:
            body()
        else:
            mine = jnp.logical_and(self.row >= self.first, self.row < self.first + self.owners)
            pl.when(mine)(body)

    def each_owner(self, body):
        @pl.loop(0, self.owners, unroll=self.nrows <= 16)
        def _(o):
            owner = lax.rem(o + self.row, self.owners)
            pl.when(self.first + owner != self.row)(lambda: body(owner))

    def pairs(self):
        for k in range(1, self.nsnaps):
            self.h_copy(self.snap, self.snap_peer(k), k).start()

    def scatter(self):
        for k in range(1, self.nsnaps):
            self.h_copy(self.snap_peer(k), self.snap, k).wait_recv()
        at = pl.ds(pl.multiple_of(self.snap * self.half, self.half), self.half)
        mine = self.part[at, :]
        for k in range(1, self.nsnaps):
            mine = mine + self.pair[self.snap_peer(k)]
        self.mine[...] = mine
        self.each_owner(lambda owner: self.g_copy(self.row, owner).start())

    def reduce(self):
        def body():
            owner = self.row - self.first
            at = pl.ds(pl.multiple_of(owner * self.chunk, self.chunk), self.chunk)

            def step(k, acc):
                src = lax.rem(self.row + self.nrows - k, self.nrows)
                self.g_copy(src, owner).wait_recv()
                return acc + self.chunks[src]

            acc = lax.fori_loop(1, self.nrows, step, self.mine[at, :], unroll=self.nrows <= 16)
            at = pl.multiple_of(self.snap * self.half + owner * self.chunk, self.chunk)
            self.result[pl.ds(at, self.chunk), :] = acc

            @pl.loop(1, self.nrows, unroll=self.nrows <= 16)
            def _(k):
                self.r_copy(owner, lax.rem(self.row + k, self.nrows)).start()

        self.if_owner(body)

    def share(self):
        self.each_owner(lambda owner: self.r_copy(owner, self.row).wait_recv())
        for k in range(1, self.nsnaps):
            self.b_copy(self.snap, self.snap_peer(k), k).start()

    def arrive(self):
        for k in range(1, self.nsnaps):
            self.b_copy(self.snap_peer(k), self.snap, k).wait_recv()

    def finish(self):
        for k in range(1, self.nsnaps):
            self.h_copy(self.snap, self.snap_peer(k), k).wait_send()
            self.b_copy(self.snap, self.snap_peer(k), k).wait_send()
        self.each_owner(lambda owner: self.g_copy(self.row, owner).wait_send())

        def body():
            @pl.loop(1, self.nrows, unroll=self.nrows <= 16)
            def _(k):
                self.r_copy(self.row - self.first, lax.rem(self.row + k, self.nrows)).wait_send()

        self.if_owner(body)


class Relay:
    def __init__(self, view, send, recv, place):
        self.view, self.send, self.recv = view, send, recv
        self.snap, self.row, self.nrows = place
        self.depth = self.nrows // PLANE
        self.level, self.place = self.row // PLANE, lax.rem(self.row, PLANE)
        side = self.place + 1 - 2 * lax.rem(self.place, 2)
        self.places = (side, PLANE - 1 - side, PLANE - 1 - self.place)

    def over(self, b, kind, at, slot, to):
        view = self.view(b)
        return remote(view, view, self.send.at[kind, slot], self.recv.at[kind, at], (self.snap, to))

    def level_copy(self, k):
        to = lax.rem(self.level + k, self.depth)
        return self.over(self.row, 0, self.level, to, to * PLANE + self.place)

    def spread(self, v):
        b = v * PLANE + self.place
        return [
            self.over(b, 1 + i, v, v, self.level * PLANE + p) for i, p in enumerate(self.places)
        ]

    def level_at(self, k):
        return lax.rem(self.level + self.depth - k, self.depth)

    def begin(self):
        @pl.loop(1, self.depth, unroll=self.depth <= 4)
        def _(k):
            self.level_copy(k).start()

        for c in self.spread(self.level):
            c.start()

    def forward(self):
        @pl.loop(1, self.depth, unroll=self.depth <= 4)
        def _(k):
            v = self.level_at(k)
            self.over(v * PLANE + self.place, 0, v, v, self.row).wait_recv()
            for c in self.spread(v):
                c.start()

    def arrive(self, v):
        for i, p in enumerate(self.places):
            self.over(v * PLANE + p, 1 + i, v, v, self.row).wait_recv()

    def finish(self):
        @pl.loop(1, self.depth, unroll=self.depth <= 4)
        def _(k):
            self.level_copy(k).wait_send()

        @pl.loop(0, self.depth)
        def _(v):
            for c in self.spread(v):
                c.wait_send()


def embed(
    nrows, nsnaps, slots,
    cols_hbm, count_hbm, tiles_hbm, x_hbm,
    left_ref, right_ref,
    cols_ref, count_ref, tiles_ref, out_tiles, in_tiles, x_all, parts, sums, s_all, image_ref,
    part0, pair0, mine0, chunks0, total0, part1, pair1, mine1, chunks1, total1,
    ready, local_sem, t_send, t_recv, p_send, p_recv, f_send, f_recv, c_send, c_recv,
    x_send0, x_recv0, x_send1, x_recv1, s_send0, s_recv0, s_send1, s_recv1, *total_sems,
):
    snap = lax.axis_index("tm")
    row = lax.axis_index("rows")
    piece = BLOCK // nsnaps
    depth = nrows // PLANE
    level = row // PLANE
    halves = range(COLS // BLOCK)

    def snap_peer(k):
        return lax.rem(snap + k, nsnaps)

    def row_peer(k):
        return lax.rem(row + k, nrows)

    barrier = pltpu.get_barrier_semaphore()

    side = row + 1 - 2 * lax.rem(row, 2)
    near = [side, level * PLANE + PLANE - 1 - lax.rem(side, PLANE)]
    near.append(level * PLANE + PLANE - 1 - lax.rem(row, PLANE))

    def greet(to):
        pl.semaphore_signal(barrier, inc=1, device_id=to, device_id_type=MESH)

    @pl.loop(1, depth)
    def _(k):
        greet((snap, row_peer(k * PLANE)))

    for r in near:
        greet((snap, r))
    for k in range(1, nsnaps):
        greet((snap_peer(k), row))

    x_in = [
        pltpu.make_async_copy(
            x_hbm.at[0, :, pl.ds(h * BLOCK, BLOCK)], x_all.at[h, row], local_sem.at[h]
        )
        for h in halves
    ]
    loads = [
        pltpu.make_async_copy(cols_hbm, cols_ref, local_sem.at[2]),
        pltpu.make_async_copy(count_hbm, count_ref, local_sem.at[3]),
        pltpu.make_async_copy(tiles_hbm.at[0], tiles_ref.at[pl.ds(0, slots)], local_sem.at[4]),
    ]
    for c in x_in + loads:
        c.start()
    tiles_ref[slots] = jnp.zeros((BLOCK, BLOCK), tiles_ref.dtype)
    for c in x_in:
        c.wait()

    spot = (snap, row, nrows)
    x_sems = ((x_send0, x_recv0), (x_send1, x_recv1))
    s_sems = ((s_send0, s_recv0), (s_send1, s_recv1))
    x_relay = [Relay(lambda b, h=h: x_all.at[h, b], *x_sems[h], spot) for h in halves]
    s_relay = [Relay(lambda b, h=h: s_all.at[h, snap, b], *s_sems[h], spot) for h in halves]

    pl.semaphore_wait(barrier, depth - 1 + len(near) + nsnaps - 1)
    for r in x_relay:
        r.begin()
    for r in near:
        pl.semaphore_signal(ready, inc=1, device_id=(snap, r), device_id_type=MESH)

    for c in loads:
        c.wait()
    live = [jnp.where(s < count_ref[0, 0], cols_ref[0, s], -1) for s in range(slots)]

    @pl.loop(0, nrows)
    def _(c):
        slot = jnp.int32(slots)
        for s in range(slots):
            slot = jnp.where(live[s] == c, s, slot)
        out_tiles[c] = tiles_ref[slot]

    in_tiles[row] = out_tiles[row]

    def t_copy(src, k):
        to = row_peer(k)
        return remote(
            out_tiles.at[to], in_tiles.at[src], t_send.at[k], t_recv.at[src], (snap, to)
        )

    pl.semaphore_wait(ready, len(near))

    @pl.loop(1, nrows, unroll=nrows <= 16)
    def _(k):
        t_copy(row, k).start()

    x_relay[0].forward()

    x_relay[1].forward()

    def p_copy(h, src, to, k):
        view = parts.at[h, src, to]
        return remote(view, view, p_send.at[h, k], p_recv.at[h, src], (to, row))

    def f_copy(h, src, to, k):
        view = sums.at[h, src]
        return remote(view, view, f_send.at[h, k], f_recv.at[h, src], (to, row))

    for h in halves:
        value = None
        for k in range(depth):
            v = lax.rem(level + depth - k, depth)
            x_relay[h].arrive(v)
            first = v * PLANE
            tiles_of = jnp.concatenate([out_tiles[first + i] for i in range(PLANE)], axis=1)
            term = dot_nn(tiles_of, x_all[h, pl.ds(first, PLANE)].reshape(PLANE * BLOCK, BLOCK))
            value = term if value is None else value + term
        parts[h, snap] = value.reshape(nsnaps, piece, BLOCK)
        for k in range(1, nsnaps):
            p_copy(h, snap, snap_peer(k), k).start()
        for k in range(1, nsnaps):
            p_copy(h, snap_peer(k), snap, k).wait_recv()
        summed = parts[h, 0, snap]
        for k in range(1, nsnaps):
            summed = summed + parts[h, k, snap]
        sums[h, snap] = summed
        s_all[h, snap, row] = summed.astype(jnp.bfloat16)
        s_relay[h].begin()

    for h in halves:
        s_relay[h].forward()

    def c_copy(h, src, v, to, k):
        view = s_all.at[h, src, pl.ds(v * PLANE, PLANE)]
        return remote(view, view, c_send.at[h, k, v], c_recv.at[h, src, v], (to, row))

    def share(h):
        @pl.loop(0, depth)
        def _(k):
            v = lax.rem(level + depth - k, depth)
            s_relay[h].arrive(v)
            for i in range(1, nsnaps):
                c_copy(h, snap, v, snap_peer(i), i).start()

    def shared(h):
        @pl.loop(0, depth)
        def _(v):
            for i in range(1, nsnaps):
                c_copy(h, snap_peer(i), v, snap, i).wait_recv()

    def s_of(h, t):
        return s_all[h, t].reshape(nrows * piece, BLOCK)

    def tiles_at(t):
        return in_tiles[:, t * piece : (t + 1) * piece, :].reshape(nrows * piece, BLOCK)

    def image_of(h):
        return functools.reduce(
            jnp.add, [dot_tn(tiles_at(t), s_of(h, t)) for t in range(nsnaps)]
        )

    def gram_of(g, h):
        return functools.reduce(jnp.add, [dot_tn(s_of(g, t), s_of(h, t)) for t in range(nsnaps)])

    where = (snap, row, nsnaps, nrows)
    first_total = Total((part0, pair0, mine0, chunks0, total0), total_sems[:8], where)
    other_total = Total((part1, pair1, mine1, chunks1, total1), total_sems[8:], where)
    lo, hi = slice(0, BLOCK), slice(BLOCK, COLS)

    share(0)

    @pl.loop(1, nrows, unroll=nrows <= 16)
    def _(k):
        t_copy(row_peer(nrows - k), k).wait_recv()

    shared(0)
    image = image_of(0)
    image_ref[0] = image
    part0[...] = dot_tn(image, image, HIGHEST)
    first_total.pairs()

    first_total.scatter()
    share(1)
    shared(1)
    image = image_of(1)
    image_ref[1] = image
    part1[lo, :] = dot_tn(image, image_ref[0], HIGHEST)
    part1[hi, :] = dot_tn(image, image, HIGHEST)
    other_total.pairs()

    for h in halves:
        for k in range(1, nsnaps):
            f_copy(h, snap, snap_peer(k), k).start()
    gram00, gram10, gram11 = gram_of(0, 0), gram_of(1, 0), gram_of(1, 1)
    other_total.scatter()
    first_total.reduce()

    upper = Elimination(gram00).run(6)
    other_total.reduce()
    upper = upper.run(8 - 6).result()
    for h in halves:
        for k in range(1, nsnaps):
            f_copy(h, snap_peer(k), snap, k).wait_recv()
    left_lo, left_hi = (sums[h].reshape(BLOCK, BLOCK) for h in halves)
    below = dot_nt(gram10, upper)
    left_head = dot_nt(left_lo, upper)
    left_tail = left_hi - dot_nt(left_head, below)
    left_lower = Elimination(gram11 - dot_nt(below, below)).run(6)
    left_scale = math.sqrt(nrows * BLOCK)
    left_ref[:, lo] = left_head * left_scale

    first_total.share()
    first_total.arrive()
    upper = Elimination(total0[...]).run(6)
    other_total.share()
    upper = upper.run(8 - 6).result()
    head = dot_nt(image_ref[0], upper)
    scale = math.sqrt(nsnaps * nrows * BLOCK)
    right_ref[:, lo] = head * scale
    other_total.arrive()
    below = dot_nt(total1[lo, :], upper)
    lower = Elimination(total1[hi, :] - dot_nt(below, below)).run().result()
    tail = image_ref[1] - dot_nt(head, below)
    right_ref[:, hi] = dot_nt(tail, lower) * scale
    left_ref[:, hi] = dot_nt(left_tail, left_lower.run(8 - 6).result()) * left_scale

    for r in x_relay + s_relay:
        r.finish()
    first_total.finish()
    other_total.finish()
    for h in halves:
        for k in range(1, nsnaps):
            p_copy(h, snap, snap_peer(k), k).wait_send()
            f_copy(h, snap, snap_peer(k), k).wait_send()

            @pl.loop(0, depth)
            def _(v):
                c_copy(h, snap, v, snap_peer(k), k).wait_send()

    @pl.loop(1, nrows, unroll=nrows <= 16)
    def _(k):
        t_copy(row, k).wait_send()


def hand_over(left_in, right_in, left_out, right_out):
    left_out[...] = left_in[...]
    right_out[...] = right_in[...]


def on_device(tiles, tile_cols, tile_count, start_right):
    nrows = lax.axis_size("rows")
    nsnaps = lax.axis_size("tm")
    slots = tiles.shape[1]
    depth = nrows // PLANE
    piece = BLOCK // nsnaps
    f32, bf16 = jnp.float32, jnp.bfloat16
    vmem = pl.BlockSpec(memory_space=pltpu.VMEM)
    hbm = pl.BlockSpec(memory_space=pltpu.HBM)
    dma = lambda *n: pltpu.SemaphoreType.DMA(n)
    block = jax.ShapeDtypeStruct((BLOCK, COLS), f32)
    params = dict(vmem_limit_bytes=60 * 1024 * 1024)
    totals, total_sems = [], []
    for size in (BLOCK, 2 * BLOCK):
        half = size // nsnaps
        owners = min(nrows, half // (8 if size == BLOCK else 16))
        totals += [
            pltpu.VMEM((size, BLOCK), f32),
            pltpu.VMEM((nsnaps, half, BLOCK), f32),
            pltpu.VMEM((half, BLOCK), f32),
            pltpu.VMEM((nrows, half // owners, BLOCK), f32),
            pltpu.VMEM((size, BLOCK), f32),
        ]
        total_sems += [dma(nsnaps), dma(nsnaps)] + [dma(nrows)] * 4 + [dma(nsnaps), dma(nsnaps)]
    left, right = pl.pallas_call(
        functools.partial(embed, nrows, nsnaps, slots),
        out_shape=(block, block),
        in_specs=[hbm] * 4,
        out_specs=(vmem, vmem),
        scratch_shapes=[
            pltpu.SMEM(tile_cols.shape, jnp.int32),
            pltpu.SMEM(tile_count.shape, jnp.int32),
            pltpu.VMEM((slots + 1, BLOCK, BLOCK), bf16),
            pltpu.VMEM((nrows, BLOCK, BLOCK), bf16),
            pltpu.VMEM((nrows, BLOCK, BLOCK), bf16),
            pltpu.VMEM((2, nrows, BLOCK, BLOCK), bf16),
            pltpu.VMEM((2, nsnaps, nsnaps, piece, BLOCK), f32),
            pltpu.VMEM((2, nsnaps, piece, BLOCK), f32),
            pltpu.VMEM((2, nsnaps, nrows, piece, BLOCK), bf16),
            pltpu.VMEM((2, BLOCK, BLOCK), f32),
            *totals,
            pltpu.SemaphoreType.REGULAR,
            dma(5), dma(nrows), dma(nrows),
            *[dma(2, nsnaps)] * 4,
            *[dma(2, nsnaps, depth)] * 2,
            *[dma(4, depth)] * 8,
            *total_sems,
        ],
        compiler_params=pltpu.CompilerParams(collective_id=0, has_side_effects=True, **params),
        name="embed",
    )(tile_cols, tile_count, tiles, start_right)
    left, right = pl.pallas_call(
        hand_over,
        out_shape=(block, block),
        in_specs=[vmem, vmem],
        out_specs=(vmem, vmem),
        compiler_params=pltpu.CompilerParams(**params),
        name="hand_over",
    )(left, right)
    return (left, right[None])


def solution(mesh):
    placed = (P("tm", "rows", None, None), P("tm", "rows"), P("tm", "rows"), P("tm", "rows", None))
    return jax.shard_map(
        on_device,
        mesh=mesh,
        in_specs=placed,
        out_specs=(P("rows", None), P("tm", "rows", None)),
        check_vma=False,
    )
```
